32 devices in a mesh: ctx: 8 (over z, core), ch: 4 (over y, x).
Axes of the slice: x: 2, y: 2, z: 4, core: 2. Of those that a mesh axis runs over, the one named last changes fastest.
Arguments:
- token_ids: int32 [1536], P('ctx'), may hold values from 0 to 511
- query_order: int32 [16], replicated, may hold values from 0 to 15, each once
- embed_table: bfloat16 [512, 8192], P(None, 'ch'), may hold values from -36 to 36
- hyena_gain: float32 [8192], P('ch'), may hold values from 0.5 to 1.5
- short_filter: float32 [3, 3, 8192], P(None, None, 'ch'), may hold values from -3 to 3
- decay_rate: float32 [16, 8192], P(None, 'ch'), may hold values from 6.510417e-05 to 0.03125
- residue: float32 [16, 8192], P(None, 'ch'), may hold values from -0.45 to 0.45
- skip_gain: float32 [8192], P('ch'), may hold values from -3 to 3
- attn_gain: float32 [8192], P('ch'), may hold values from 0.5 to 1.5
- w_qkv: bfloat16 [8192, 1536], P('ctx', 'ch'), may hold values from -0.243067956 to 0.243067956
Outputs:
- mixed: bfloat16 [1536, 8192], P('ctx', 'ch')
- attended: bfloat16 [1536, 512], P('ctx', 'ch')
The draws below stay inside these ranges and needn't reach their ends.
Inputs may be any that keep to these rules, and one draw needn't show every extreme that they name: `query_order`: each of the 16 half-blocks of 96 positions is named exactly once.
All inputs are finite; a program needn't handle non-finite values.
Results may differ from the reference program's by a relative error of at most 0.0085.
Values may be sent and summed in bfloat16 or wider, within the bound.
A program may use at most 192 MiB of HBM per device.

```python
import math
import jax
import jax.numpy as jnp
import numpy as np
from jax import lax

D = 8192
VOCAB = 512
HEAD_DIM = 128
HEAD_DEV = 1
ORDER = 16
SHORT = 3
HEADS = 4
SEQ = 1536
HALF = 96
BLOCKS = 16


def modal_draw(key):
    rate_key = jax.random.fold_in(key, 101)
    weight_key = jax.random.fold_in(key, 303)
    lowest = math.log(0.1 / SEQ)
    highest = math.log(1.0 / 32.0)
    spread = jax.random.uniform(rate_key, (ORDER, D), jnp.float32)
    rates = jnp.exp(lowest + spread * (highest - lowest))
    weights = jax.random.truncated_normal(weight_key, -3.0, 3.0, (ORDER, D), jnp.float32) * jnp.sqrt(2.0 * rates) * 0.6
    return (rates, weights)


def draw_decay_rate(key, part):
    return modal_draw(key)[0]


def draw_residue(key, part):
    return modal_draw(key)[1]


def draw_embed_table(key, part):
    row_key = jax.random.fold_in(key, 11)
    column_key = jax.random.fold_in(key, 12)
    value_key = jax.random.fold_in(key, 13)
    position = jnp.arange(D, dtype=jnp.float32) / D
    row_scale = jnp.exp(jax.random.uniform(row_key, (VOCAB, 1), jnp.float32) * math.log(10.0)) * 0.3
    jitter = jnp.exp(jax.random.uniform(column_key, (1, D), jnp.float32) * math.log(1.0 / 3.0))
    column_scale = (3.0 ** position)[None, :] * jitter
    entries = jax.random.truncated_normal(value_key, -4.0, 4.0, (VOCAB, D), jnp.float32)
    return (entries * row_scale * column_scale).astype(jnp.bfloat16)


def draw_w_qkv(key, part):
    width = HEAD_DEV * HEAD_DIM
    groups = HEADS // HEAD_DEV
    base = jax.random.truncated_normal(key, -4.0, 4.0, (D, groups, 3, width), jnp.float32) / math.sqrt(D)
    query_part = base[:, :, 0]
    key_part = base[:, :, 1]
    value_part = base[:, :, 2]
    stacked = jnp.stack([query_part, key_part, value_part], axis=2)
    return stacked.reshape(D, groups * 3 * width).astype(jnp.bfloat16)


def place_ends(result, own_key, least, top_value):
    dims = result.shape
    spot = [jax.random.randint(jax.random.fold_in(own_key, axis), (), 0, dims[axis]) for axis in range(len(dims))]
    result = result.at[tuple(spot)].set(least)
    longest = dims.index(max(dims))
    spot[longest] = (spot[longest] + 1) % dims[longest]
    return result.at[tuple(spot)].set(top_value)


def block_levels(stream_key, dims, split, smallest, largest):
    level = 1.0
    for dim, parts in split:
        heights = jax.random.uniform(jax.random.fold_in(jax.random.fold_in(stream_key, 6), dim), (parts,), jnp.float32, smallest / len(split), largest / len(split))
        level = level * jnp.repeat(jnp.exp(heights), dims[dim] // parts).reshape((-1,) + (1,) * (len(dims) - 1 - dim))
    return level


def cumulative_ranks(count, slope):
    loads = [(1 << 20) // math.isqrt(standing ** slope) + 1 for standing in range(1, count + 1)]
    scale = 1 + sum(loads) // (1 << 30)
    return np.cumsum(np.array([max(1, weight // scale) for weight in loads]))


def ranked_ids(own_key, dims, number_of, slope):
    table = cumulative_ranks(number_of, slope)
    lot = jax.random.randint(jax.random.fold_in(own_key, 1), dims, 0, int(table[number_of - 1]))
    grade = jnp.searchsorted(jnp.asarray(table, jnp.int32), lot, side="right")
    return jax.random.permutation(jax.random.fold_in(own_key, 2), number_of)[grade].astype(jnp.int32)


def scatter_about(rng, shape, scale, reach, shards=(), held_as=jnp.bfloat16):
    loudness = block_levels(rng, shape, shards, -0.22, 0.18) if shards else 1.0
    drawn = jax.random.normal(rng, shape, jnp.float32) * scale * loudness
    return jnp.minimum(jnp.maximum(drawn, -reach), reach).astype(held_as)


def setup_inputs(seed: int = 0) -> dict:
    key_list = jax.random.split(jax.random.key(seed), 11)
    token_ids = place_ends(ranked_ids(key_list[0], (SEQ,), VOCAB, 2), jax.random.fold_in(key_list[0], 3), 0, VOCAB - 1).astype(jnp.int32)
    query_order = jax.random.permutation(key_list[1], BLOCKS).astype(jnp.int32)
    embed_table = draw_embed_table(jax.random.fold_in(key_list[10], 71), 0)
    hyena_gain = jnp.clip(1.0 + 0.1 * jax.random.normal(key_list[3], (D,), jnp.float32), 0.5, 1.5)
    short_filter = scatter_about(key_list[4], (3, SHORT, D), 0.6, 3.0, ((2, 4),), jnp.float32)
    decay_rate = draw_decay_rate(jax.random.fold_in(key_list[10], 71), 0)
    residue = draw_residue(jax.random.fold_in(key_list[10], 71), 0)
    skip_gain = scatter_about(key_list[7], (D,), 1.0, 3.0, ((0, 4),), jnp.float32)
    attn_gain = jnp.clip(1.0 + 0.1 * jax.random.normal(key_list[8], (D,), jnp.float32), 0.5, 1.5)
    w_qkv = draw_w_qkv(jax.random.fold_in(key_list[10], 71), 0)
    return dict(token_ids=token_ids, query_order=query_order, embed_table=embed_table, hyena_gain=hyena_gain, short_filter=short_filter, decay_rate=decay_rate, residue=residue, skip_gain=skip_gain, attn_gain=attn_gain, w_qkv=w_qkv)


def rms_scale(values, gain_vector):
    mean_square = lax.optimization_barrier(jnp.mean(values * values, axis=1, keepdims=True))
    return values * lax.rsqrt(mean_square + 1e-06) * gain_vector[None, :]

def rotary(vectors, positions):
    half_dim = vectors.shape[-1] // 2
    frequency = 10000.0 ** (-(jnp.arange(half_dim, dtype=jnp.float32) / half_dim))
    angle = positions.astype(jnp.float32)[:, None] * frequency[None, :]
    cosine = jnp.cos(angle)[:, None, :]
    sine = jnp.sin(angle)[:, None, :]
    first = vectors[..., :half_dim]
    second = vectors[..., half_dim:]
    return jnp.concatenate([first * cosine - second * sine, second * cosine + first * sine], axis=-1)

def long_filter(gated, decay_rate, residue):
    sub_length = 32
    highest = lax.Precision.HIGHEST
    lag_values = jnp.arange(sub_length, dtype=jnp.float32)
    lag_decay = jnp.exp(-decay_rate[None] * lag_values[:, None, None])
    filter_taps = lax.optimization_barrier(jnp.sum(lag_decay * residue[None], axis=1))
    offsets = jnp.arange(sub_length, dtype=jnp.int32)[:, None] - jnp.arange(sub_length, dtype=jnp.int32)[None, :]
    toeplitz = jnp.where((offsets >= 0)[:, :, None], filter_taps[jnp.clip(offsets, 0, sub_length - 1)], 0.0)
    end_decay = jnp.exp(-decay_rate[None] * (sub_length - 1 - lag_values)[:, None, None])
    entry_weight = residue[None] * jnp.exp(-decay_rate[None] * (lag_values + 1.0)[:, None, None])
    step_decay = jnp.exp(-decay_rate * float(sub_length))

    def advance(state, block_values):
        inside = jnp.einsum('tsc,sc->tc', toeplitz, block_values, precision=highest)
        across = jnp.einsum('nc,tnc->tc', state, entry_weight, precision=highest)
        sub_end = jnp.einsum('sc,snc->nc', block_values, end_decay, precision=highest)
        return (step_decay * state + sub_end, inside + across)
    pieces = gated.reshape(SEQ // sub_length, sub_length, D)
    initial = jnp.zeros((ORDER, D), jnp.float32)
    _, responses = lax.scan(advance, initial, pieces)
    return responses.reshape(SEQ, D)

def reference(token_ids, query_order, embed_table, hyena_gain, short_filter, decay_rate, residue, skip_gain, attn_gain, w_qkv):
    highest = lax.Precision.HIGHEST
    embedded = embed_table[token_ids]
    embedded_wide = embedded.astype(jnp.float32)
    hyena_normed = rms_scale(embedded_wide, hyena_gain).astype(jnp.bfloat16)
    padded = jnp.concatenate([jnp.zeros((SHORT - 1, D), jnp.bfloat16), hyena_normed], axis=0).astype(jnp.float32)
    streams = []
    for stream_index in range(3):
        accum = jnp.zeros((SEQ, D), jnp.float32)
        for tap_index in range(SHORT):
            begin = SHORT - 1 - tap_index
            accum = accum + short_filter[stream_index, tap_index][None, :] * padded[begin:begin + SEQ]
        streams.append(accum)
    gated = streams[1] * streams[2]
    long_response = long_filter(gated, decay_rate, residue)
    mixed = (embedded_wide + streams[0] * (long_response + skip_gain[None, :] * gated)).astype(jnp.bfloat16)
    attn_normed = rms_scale(mixed.astype(jnp.float32), attn_gain).astype(jnp.bfloat16)
    width = HEAD_DEV * HEAD_DIM
    groups = HEADS // HEAD_DEV
    projected = jnp.dot(attn_normed, w_qkv, preferred_element_type=jnp.float32).reshape(SEQ, groups, 3 * width)
    positions = jnp.arange(SEQ, dtype=jnp.int32)
    heads_all = HEADS
    queries = rotary(projected[:, :, :width].reshape(SEQ, heads_all, HEAD_DIM), positions).astype(jnp.bfloat16)
    keys = rotary(projected[:, :, width:2 * width].reshape(SEQ, heads_all, HEAD_DIM), positions).astype(jnp.bfloat16)
    values = projected[:, :, 2 * width:].reshape(SEQ, heads_all, HEAD_DIM).astype(jnp.bfloat16)
    keys_wide = jnp.transpose(keys, (1, 0, 2)).astype(jnp.float32)
    values_wide = jnp.transpose(values, (1, 0, 2)).astype(jnp.float32)
    scale = 1.0 / math.sqrt(HEAD_DIM)
    query_rows = 256

    def attend(block_index):
        start = block_index * query_rows
        query_block = lax.dynamic_slice_in_dim(queries, start, query_rows, 0)
        query_block = jnp.transpose(query_block, (1, 0, 2)).astype(jnp.float32)
        scores = jnp.einsum('hqd,hkd->hqk', query_block, keys_wide, precision=highest) * scale
        query_positions = start + jnp.arange(query_rows, dtype=jnp.int32)
        allowed = (positions[None, :] <= query_positions[:, None])[None]
        masked = jnp.where(allowed, scores, -1e+30)
        top = lax.optimization_barrier(jnp.max(masked, axis=-1, keepdims=True))
        weights = jnp.where(allowed, jnp.exp(masked - top), 0.0)
        total = lax.optimization_barrier(jnp.sum(weights, axis=-1))
        rounded = lax.optimization_barrier(weights.astype(jnp.bfloat16)).astype(jnp.float32)
        context = jnp.einsum('hqk,hkd->hqd', rounded, values_wide, precision=highest) / total[..., None]
        return jnp.transpose(context, (1, 0, 2)).reshape(query_rows, heads_all * HEAD_DIM).astype(jnp.bfloat16)
    blocks_out = lax.map(attend, jnp.arange(SEQ // query_rows, dtype=jnp.int32))
    contexts = blocks_out.reshape(SEQ, heads_all * HEAD_DIM)
    attended = contexts.reshape(BLOCKS, HALF, heads_all * HEAD_DIM)[query_order].reshape(SEQ, heads_all * HEAD_DIM)
    return (mixed, attended)
```

```python
import functools
import math

import jax
import jax.numpy as jnp
from jax import lax
from jax.experimental import pallas as pl
from jax.experimental.pallas import tpu as pltpu
from jax.sharding import PartitionSpec as P

D = 8192
HEAD_DIM = 128
HEAD_DEV = 1
SHORT = 3
ORDER = 16
HALO = 16
SPAN_MOST = 1024


def modal_local(
    ids_ref,
    scale_ref,
    table_ref,
    gain_ref,
    taps_ref,
    decay_ref,
    residue_ref,
    skip_ref,
    query_ref,
    base_ref,
    state_ref,
    normed_ref,
    gated_ref,
    long_ref,
):
    rows = query_ref.shape[0]
    vocab, span = table_ref.shape
    tiles = span // 128
    padded = ids_ref.shape[0]
    onehot = (
        (ids_ref[...] == lax.broadcasted_iota(jnp.int32, (padded, vocab), 1))
        .astype(jnp.float32)
        .astype(jnp.bfloat16)
    )
    embedded = jnp.dot(onehot, table_ref[...], preferred_element_type=jnp.float32)
    base_ref[...] = embedded[HALO:]
    normed_ref[...] = (
        (embedded * scale_ref[...] * gain_ref[...]).astype(jnp.bfloat16).astype(jnp.float32)
    )
    taps = taps_ref[...]

    def stream(j):
        total = taps[3 * j : 3 * j + 1] * normed_ref[HALO:]
        for i in range(1, SHORT):
            k = 3 * j + i
            total = total + taps[k : k + 1] * normed_ref[HALO - i : HALO - i + rows]
        return total

    query = stream(0)
    gated = stream(1) * stream(2)
    query_ref[...] = query
    base_ref[...] += query * (skip_ref[...] * gated)
    for r in range(rows // 8):
        for k in range(tiles):
            gated_ref[(r * tiles + k) * 8 : (r * tiles + k + 1) * 8, :] = gated[
                r * 8 : r * 8 + 8, k * 128 : k * 128 + 128
            ]
    decay = [jnp.exp(-decay_ref[n]) for n in range(ORDER)]

    def step(r, states):
        states = list(states)
        for t in range(8):
            place = pl.ds(r * (8 * tiles) + t, tiles, stride=8)
            entry = gated_ref[place, :]
            terms = []
            for n in range(ORDER):
                states[n] = decay[n] * states[n] + entry
                terms.append(residue_ref[n] * states[n])
            while len(terms) > 1:
                terms = [a + b for a, b in zip(terms[::2], terms[1::2])]
            long_ref[place, :] = terms[0]
        return tuple(states)

    zero = jnp.zeros((tiles, 128), jnp.float32)
    states = lax.fori_loop(0, rows // 8, step, (zero,) * ORDER)
    for n in range(ORDER):
        state_ref[n] = states[n]
    for r in range(rows // 8):
        for k in range(tiles):
            spot = (slice(r * 8, r * 8 + 8), slice(k * 128, k * 128 + 128))
            base_ref[spot] += (
                query_ref[spot] * long_ref[(r * tiles + k) * 8 : (r * tiles + k + 1) * 8, :]
            )


def modal_finish(
    rank_ref,
    states_ref,
    decay_ref,
    residue_ref,
    query_ref,
    base_ref,
    gain_ref,
    mixed_ref,
    scaled_ref,
    energy_ref,
    long_ref,
):
    rows, span = query_ref.shape
    tiles = span // 128
    rank = rank_ref[0]
    block_decay = [jnp.exp(-decay_ref[n] * float(rows)) for n in range(ORDER)]

    def carry(k, states):
        return tuple(states[n] * block_decay[n] + states_ref[k, n] for n in range(ORDER))

    zero = jnp.zeros((tiles, 128), jnp.float32)
    incoming = lax.fori_loop(0, rank, carry, (zero,) * ORDER)
    decay = [jnp.exp(-decay_ref[n]) for n in range(ORDER)]

    def step(r, terms):
        terms = list(terms)
        for t in range(8):
            terms = [decay[n] * terms[n] for n in range(ORDER)]
            sums = terms
            while len(sums) > 1:
                sums = [a + b for a, b in zip(sums[::2], sums[1::2])]
            long_ref[pl.ds(r * (8 * tiles) + t, tiles, stride=8), :] = sums[0]
        return tuple(terms)

    lax.fori_loop(
        0, rows // 8, step, tuple(residue_ref[n] * incoming[n] for n in range(ORDER))
    )
    @pl.when(pl.program_id(0) == 0)
    def _():
        energy_ref[...] = jnp.zeros_like(energy_ref)

    for r in range(rows // 16):
        energy = jnp.zeros((16, 128), jnp.float32)
        for k in range(tiles):
            spot = (slice(r * 16, r * 16 + 16), slice(k * 128, k * 128 + 128))
            first = (2 * r * tiles + k) * 8
            second = ((2 * r + 1) * tiles + k) * 8
            late = jnp.concatenate(
                [long_ref[first : first + 8, :], long_ref[second : second + 8, :]], axis=0
            )
            mixed = (base_ref[spot] + query_ref[spot] * late).astype(jnp.bfloat16)
            mixed_ref[spot] = mixed
            wide = mixed.astype(jnp.float32)
            scaled_ref[spot] = (wide * gain_ref[:, spot[1]]).astype(jnp.bfloat16)
            energy = energy + wide * wide
        energy_ref[r * 16 : r * 16 + 16, :] += energy


def attend(blocks_ref, qkv_ref, out_ref):
    half_rows = out_ref.shape[0] // 2
    keys_total = qkv_ref.shape[0]
    width = HEAD_DIM
    for b in range(2):
        start = pl.multiple_of(blocks_ref[b] * half_rows, 32)
        queries = qkv_ref[pl.ds(start, half_rows), :width]
        keys = qkv_ref[:, width : 2 * width]
        values = qkv_ref[:, 2 * width :]
        scores = lax.dot_general(
            queries, keys, (((1,), (1,)), ((), ())), preferred_element_type=jnp.float32
        ) * (1.0 / math.sqrt(HEAD_DIM))
        at = start + lax.broadcasted_iota(jnp.int32, (half_rows, keys_total), 0)
        allowed = lax.broadcasted_iota(jnp.int32, (half_rows, keys_total), 1) <= at
        masked = jnp.where(allowed, scores, -1e30)
        top = jnp.max(masked, axis=1, keepdims=True)
        weights = jnp.where(allowed, jnp.exp(masked - top), 0.0)
        total = jnp.sum(weights, axis=1, keepdims=True)
        out = jnp.dot(weights.astype(jnp.bfloat16), values, preferred_element_type=jnp.float32)
        out_ref[b * half_rows : (b + 1) * half_rows, :] = (out / total).astype(jnp.bfloat16)


def rotate(vectors, cosine, sine):
    half_dim = HEAD_DIM // 2
    first = vectors[:, :half_dim]
    second = vectors[:, half_dim:]
    return jnp.concatenate(
        [first * cosine - second * sine, second * cosine + first * sine], axis=1
    )


def shards(
    token_ids,
    query_order,
    embed_table,
    hyena_gain,
    short_filter,
    decay_rate,
    residue,
    skip_gain,
    attn_gain,
    w_qkv,
):
    length = token_ids.shape[0]
    vocab = embed_table.shape[0]
    here = embed_table.shape[1]
    span = min(SPAN_MOST, here)
    spans = here // span
    tiles = span // 128
    nctx = lax.axis_size("ctx")
    rank = lax.axis_index("ctx")
    padded = length + HALO
    weights_full = lax.all_gather(w_qkv, "ctx", axis=0, tiled=True)
    earlier_ids = lax.ppermute(
        token_ids[length - HALO :], "ctx", [(i, i + 1) for i in range(nctx - 1)]
    )
    ids = jnp.concatenate([earlier_ids, token_ids])
    table_wide = embed_table.astype(jnp.float32)
    table_energy = lax.psum(jnp.sum(table_wide * table_wide, axis=1), "ch")
    energy = jnp.sum(
        jnp.where(
            ids[:, None] == jnp.arange(vocab, dtype=jnp.int32)[None, :], table_energy[None, :], 0.0
        ),
        axis=1,
    )
    real = (jnp.arange(padded) >= HALO) | (rank > 0)
    scale = jnp.where(real, lax.rsqrt(energy / D + 1e-06), 0.0)
    decay_tiles = decay_rate.reshape(ORDER, spans, tiles, 128).swapaxes(0, 1)
    residue_tiles = residue.reshape(ORDER, spans, tiles, 128).swapaxes(0, 1)
    row = lambda size: pl.BlockSpec((size, span), lambda h: (0, h))
    tile = pl.BlockSpec((None, ORDER, tiles, 128), lambda h: (h, 0, 0, 0))
    lone = lambda size: pl.BlockSpec((size, 1), lambda h: (0, 0))
    query, base, state = pl.pallas_call(
        modal_local,
        grid=(spans,),
        in_specs=[
            lone(padded), lone(padded), row(vocab), row(1), row(9), tile, tile, row(1)
        ],
        out_specs=[row(length), row(length), tile],
        out_shape=[
            jax.ShapeDtypeStruct((length, here), jnp.float32),
            jax.ShapeDtypeStruct((length, here), jnp.float32),
            jax.ShapeDtypeStruct((spans, ORDER, tiles, 128), jnp.float32),
        ],
        scratch_shapes=[
            pltpu.VMEM((padded, span), jnp.float32),
            pltpu.VMEM((length * tiles, 128), jnp.float32),
            pltpu.VMEM((length * tiles, 128), jnp.float32),
        ],
        name="modal_local",
    )(
        ids[:, None],
        scale[:, None],
        embed_table,
        hyena_gain[None],
        short_filter.reshape(9, here),
        decay_tiles,
        residue_tiles,
        skip_gain[None],
    )
    states = lax.all_gather(state, "ctx")
    mixed, scaled, lanes = pl.pallas_call(
        modal_finish,
        grid_spec=pltpu.PrefetchScalarGridSpec(
            num_scalar_prefetch=1,
            grid=(spans,),
            in_specs=[
                pl.BlockSpec((nctx, None, ORDER, tiles, 128), lambda h, s: (0, h, 0, 0, 0)),
                pl.BlockSpec((None, ORDER, tiles, 128), lambda h, s: (h, 0, 0, 0)),
                pl.BlockSpec((None, ORDER, tiles, 128), lambda h, s: (h, 0, 0, 0)),
                pl.BlockSpec((length, span), lambda h, s: (0, h)),
                pl.BlockSpec((length, span), lambda h, s: (0, h)),
                pl.BlockSpec((1, span), lambda h, s: (0, h)),
            ],
            out_specs=[
                pl.BlockSpec((length, span), lambda h, s: (0, h)),
                pl.BlockSpec((length, span), lambda h, s: (0, h)),
                pl.BlockSpec((length, 128), lambda h, s: (0, 0)),
            ],
            scratch_shapes=[pltpu.VMEM((length * tiles, 128), jnp.float32)],
        ),
        out_shape=[
            jax.ShapeDtypeStruct((length, here), jnp.bfloat16),
            jax.ShapeDtypeStruct((length, here), jnp.bfloat16),
            jax.ShapeDtypeStruct((length, 128), jnp.float32),
        ],
        name="modal_finish",
    )(rank[None], states, decay_tiles, residue_tiles, query, base, attn_gain[None])
    stream_energy = lax.psum(jnp.sum(lanes, axis=1), "ch")
    row_scale = lax.rsqrt(stream_energy / D + 1e-06)[:, None]
    scaled_full = lax.all_gather(scaled, "ch", axis=1, tiled=True)
    projected = (
        jnp.dot(scaled_full, weights_full, preferred_element_type=jnp.float32) * row_scale
    )
    half_dim = HEAD_DIM // 2
    positions = rank * length + jnp.arange(length, dtype=jnp.int32)
    frequency = 10000.0 ** (-(jnp.arange(half_dim, dtype=jnp.float32) / half_dim))
    angle = positions.astype(jnp.float32)[:, None] * frequency[None, :]
    cosine, sine = jnp.cos(angle), jnp.sin(angle)
    width = HEAD_DIM
    qkv = jnp.concatenate(
        [
            rotate(projected[:, :width], cosine, sine),
            rotate(projected[:, width : 2 * width], cosine, sine),
            projected[:, 2 * width :],
        ],
        axis=1,
    ).astype(jnp.bfloat16)
    every = lax.all_gather(qkv, "ctx", axis=0, tiled=True)
    blocks = lax.dynamic_slice_in_dim(query_order, rank * 2, 2)
    attended = pl.pallas_call(
        attend,
        in_specs=[
            pl.BlockSpec(memory_space=pltpu.SMEM),
            pl.BlockSpec(memory_space=pltpu.VMEM),
        ],
        out_specs=pl.BlockSpec(memory_space=pltpu.VMEM),
        out_shape=jax.ShapeDtypeStruct((length, width), jnp.bfloat16),
        name="attend",
    )(blocks, every)
    return (mixed, attended)


def solution(mesh):
    placed = (
        P("ctx"),
        P(),
        P(None, "ch"),
        P("ch"),
        P(None, None, "ch"),
        P(None, "ch"),
        P(None, "ch"),
        P("ch"),
        P("ch"),
        P("ctx", "ch"),
    )
    return jax.shard_map(
        shards,
        mesh=mesh,
        in_specs=placed,
        out_specs=(P("ctx", "ch"), P("ctx", "ch")),
        check_vma=False,
    )
```

```python
import functools
import math

import jax
import jax.numpy as jnp
from jax import lax
from jax.experimental import pallas as pl
from jax.experimental.pallas import tpu as pltpu
from jax.sharding import PartitionSpec as P

D = 8192
HEAD_DIM = 128
SHORT = 3
ORDER = 16
HALO = 16
SPAN_MOST = 1024


def modal_local(
    ids_ref,
    scale_ref,
    table_ref,
    gain_ref,
    taps_ref,
    decay_ref,
    residue_ref,
    skip_ref,
    query_ref,
    base_ref,
    state_ref,
    normed_ref,
    gated_ref,
    long_ref,
):
    rows = query_ref.shape[0]
    vocab, span = table_ref.shape
    tiles = span // 128
    padded = ids_ref.shape[0]
    onehot = (
        (ids_ref[...] == lax.broadcasted_iota(jnp.int32, (padded, vocab), 1))
        .astype(jnp.float32)
        .astype(jnp.bfloat16)
    )
    embedded = jnp.dot(onehot, table_ref[...], preferred_element_type=jnp.float32)
    base_ref[...] = embedded[HALO:]
    normed_ref[...] = (
        (embedded * scale_ref[...] * gain_ref[...]).astype(jnp.bfloat16).astype(jnp.float32)
    )
    taps = taps_ref[...]

    def stream(j):
        total = taps[3 * j : 3 * j + 1] * normed_ref[HALO:]
        for i in range(1, SHORT):
            k = 3 * j + i
            total = total + taps[k : k + 1] * normed_ref[HALO - i : HALO - i + rows]
        return total

    query = stream(0)
    gated = stream(1) * stream(2)
    query_ref[...] = query
    base_ref[...] += query * (skip_ref[...] * gated)
    for r in range(rows // 8):
        for k in range(tiles):
            gated_ref[(r * tiles + k) * 8 : (r * tiles + k + 1) * 8, :] = gated[
                r * 8 : r * 8 + 8, k * 128 : k * 128 + 128
            ]
    decay = [jnp.exp(-decay_ref[n]) for n in range(ORDER)]

    def step(r, states):
        states = list(states)
        for t in range(8):
            place = pl.ds(r * (8 * tiles) + t, tiles, stride=8)
            entry = gated_ref[place, :]
            terms = []
            for n in range(ORDER):
                states[n] = decay[n] * states[n] + entry
                terms.append(residue_ref[n] * states[n])
            while len(terms) > 1:
                terms = [a + b for a, b in zip(terms[::2], terms[1::2])]
            long_ref[place, :] = terms[0]
        return tuple(states)

    zero = jnp.zeros((tiles, 128), jnp.float32)
    states = lax.fori_loop(0, rows // 8, step, (zero,) * ORDER)
    for n in range(ORDER):
        state_ref[n] = states[n]
    for r in range(rows // 8):
        for k in range(tiles):
            spot = (slice(r * 8, r * 8 + 8), slice(k * 128, k * 128 + 128))
            base_ref[spot] += (
                query_ref[spot] * long_ref[(r * tiles + k) * 8 : (r * tiles + k + 1) * 8, :]
            )


def modal_finish(
    rank_ref,
    states_ref,
    decay_ref,
    residue_ref,
    query_ref,
    base_ref,
    gain_ref,
    mixed_ref,
    scaled_ref,
    energy_ref,
    long_ref,
):
    rows, span = query_ref.shape
    tiles = span // 128
    rank = rank_ref[0]
    block_decay = [jnp.exp(-decay_ref[n] * float(rows)) for n in range(ORDER)]

    def carry(k, states):
        return tuple(states[n] * block_decay[n] + states_ref[k, n] for n in range(ORDER))

    zero = jnp.zeros((tiles, 128), jnp.float32)
    incoming = lax.fori_loop(0, rank, carry, (zero,) * ORDER)
    decay = [jnp.exp(-decay_ref[n]) for n in range(ORDER)]

    def step(r, terms):
        terms = list(terms)
        for t in range(8):
            terms = [decay[n] * terms[n] for n in range(ORDER)]
            sums = terms
            while len(sums) > 1:
                sums = [a + b for a, b in zip(sums[::2], sums[1::2])]
            long_ref[pl.ds(r * (8 * tiles) + t, tiles, stride=8), :] = sums[0]
        return tuple(terms)

    lax.fori_loop(
        0, rows // 8, step, tuple(residue_ref[n] * incoming[n] for n in range(ORDER))
    )

    @pl.when(pl.program_id(0) == 0)
    def _():
        energy_ref[...] = jnp.zeros_like(energy_ref)

    for r in range(rows // 16):
        energy = jnp.zeros((16, 128), jnp.float32)
        for k in range(tiles):
            spot = (slice(r * 16, r * 16 + 16), slice(k * 128, k * 128 + 128))
            first = (2 * r * tiles + k) * 8
            second = ((2 * r + 1) * tiles + k) * 8
            late = jnp.concatenate(
                [long_ref[first : first + 8, :], long_ref[second : second + 8, :]], axis=0
            )
            mixed = (base_ref[spot] + query_ref[spot] * late).astype(jnp.bfloat16)
            mixed_ref[spot] = mixed
            wide = mixed.astype(jnp.float32)
            scaled_ref[spot] = (wide * gain_ref[:, spot[1]]).astype(jnp.bfloat16)
            energy = energy + wide * wide
        energy_ref[r * 16 : r * 16 + 16, :] += energy


def direct_kernel(axis, columns, count, *refs):
    ins, outs = refs[:count], refs[count : 2 * count]
    send, recv, own = refs[2 * count :]
    size, me = lax.axis_size(axis), lax.axis_index(axis)
    barrier = pltpu.get_barrier_semaphore()
    for d in range(1, size):
        peer = lax.rem(me + d, size)
        pl.semaphore_signal(
            barrier, inc=1, device_id={axis: peer}, device_id_type=pl.DeviceIdType.MESH
        )
    pl.semaphore_wait(barrier, size - 1)
    copies = []
    for a in range(count):
        if columns[a]:
            width = ins[a].shape[1]
            spot = outs[a].at[:, pl.ds(pl.multiple_of(me * width, 128), width)]
        else:
            spot = outs[a].at[me]
        for d in range(1, size):
            copies.append(
                pltpu.make_async_remote_copy(
                    src_ref=ins[a],
                    dst_ref=spot,
                    send_sem=send.at[a, d - 1],
                    recv_sem=recv.at[a, d - 1],
                    device_id={axis: lax.rem(me + d, size)},
                    device_id_type=pl.DeviceIdType.MESH,
                )
            )
        copies.append(pltpu.make_async_copy(ins[a], spot, own.at[a]))
    for copy in copies:
        copy.start()
    for copy in copies:
        copy.wait()


def paired_kernel(axis, in_ref, out_ref, send, recv, hand_send, hand_recv, own):
    size, me = lax.axis_size(axis), lax.axis_index(axis)
    chips = size // 2
    chip, core = lax.div(me, 2), lax.rem(me, 2)
    sibling = me + 1 - 2 * core
    peers = [sibling] + [lax.rem(chip + d, chips) * 2 + core for d in range(1, chips)]
    barrier = pltpu.get_barrier_semaphore()
    for peer in peers:
        pl.semaphore_signal(
            barrier, inc=1, device_id={axis: peer}, device_id_type=pl.DeviceIdType.MESH
        )
    pl.semaphore_wait(barrier, chips)
    copies = [
        pltpu.make_async_remote_copy(
            src_ref=in_ref,
            dst_ref=out_ref.at[me],
            send_sem=send.at[d],
            recv_sem=recv.at[d],
            device_id={axis: peers[d]},
            device_id_type=pl.DeviceIdType.MESH,
        )
        for d in range(chips)
    ]
    for copy in copies[1:]:
        copy.start()
    copies[0].start()
    mine = pltpu.make_async_copy(in_ref, out_ref.at[me], own)
    mine.start()
    hands = []
    for d in range(1, chips):
        copies[d].wait_recv()
        source = lax.rem(chip + chips - d, chips) * 2 + core
        hand = pltpu.make_async_remote_copy(
            src_ref=out_ref.at[source],
            dst_ref=out_ref.at[source],
            send_sem=hand_send.at[d],
            recv_sem=hand_recv.at[d],
            device_id={axis: sibling},
            device_id_type=pl.DeviceIdType.MESH,
        )
        hand.start()
        hands.append(hand)
    mine.wait()
    copies[0].wait_recv()
    for copy in copies:
        copy.wait_send()
    for hand in hands:
        hand.wait()


def gather_direct(axis, arrays, columns, collective_id):
    size, count = lax.axis_size(axis), len(arrays)
    vmem = pl.BlockSpec(memory_space=pltpu.VMEM)
    dma = pltpu.SemaphoreType.DMA
    return pl.pallas_call(
        functools.partial(direct_kernel, axis, columns, count),
        in_specs=[vmem] * count,
        out_specs=[vmem] * count,
        out_shape=[
            jax.ShapeDtypeStruct(
                (a.shape[0], size * a.shape[1]) if wide else (size,) + a.shape, a.dtype
            )
            for a, wide in zip(arrays, columns)
        ],
        scratch_shapes=[dma((count, size - 1)), dma((count, size - 1)), dma((count,))],
        compiler_params=pltpu.CompilerParams(
            collective_id=collective_id, has_side_effects=True
        ),
    )(*arrays)


def gather_paired(axis, array, collective_id):
    size = lax.axis_size(axis)
    vmem = pl.BlockSpec(memory_space=pltpu.VMEM)
    dma = pltpu.SemaphoreType.DMA
    chips = size // 2
    return pl.pallas_call(
        functools.partial(paired_kernel, axis),
        in_specs=[vmem],
        out_specs=vmem,
        out_shape=jax.ShapeDtypeStruct((size,) + array.shape, array.dtype),
        scratch_shapes=[dma((chips,)), dma((chips,)), dma((chips,)), dma((chips,)), dma(())],
        compiler_params=pltpu.CompilerParams(
            collective_id=collective_id, has_side_effects=True
        ),
    )(array)


def packed(vector):
    wide = -(-vector.shape[0] // 1024) * 1024
    return jnp.pad(vector, (0, wide - vector.shape[0])).reshape(wide // 128, 128)


def attend(blocks_ref, qkv_ref, out_ref):
    half_rows = out_ref.shape[0] // 2
    keys_total = qkv_ref.shape[0]
    width = HEAD_DIM
    for b in range(2):
        start = pl.multiple_of(blocks_ref[b] * half_rows, 32)
        queries = qkv_ref[pl.ds(start, half_rows), :width]
        keys = qkv_ref[:, width : 2 * width]
        values = qkv_ref[:, 2 * width :]
        scores = lax.dot_general(
            queries, keys, (((1,), (1,)), ((), ())), preferred_element_type=jnp.float32
        ) * (1.0 / math.sqrt(HEAD_DIM))
        at = start + lax.broadcasted_iota(jnp.int32, (half_rows, keys_total), 0)
        allowed = lax.broadcasted_iota(jnp.int32, (half_rows, keys_total), 1) <= at
        masked = jnp.where(allowed, scores, -1e30)
        top = jnp.max(masked, axis=1, keepdims=True)
        weights = jnp.where(allowed, jnp.exp(masked - top), 0.0)
        total = jnp.sum(weights, axis=1, keepdims=True)
        out = jnp.dot(weights.astype(jnp.bfloat16), values, preferred_element_type=jnp.float32)
        out_ref[b * half_rows : (b + 1) * half_rows, :] = (out / total).astype(jnp.bfloat16)


def rotate(vectors, cosine, sine):
    half_dim = HEAD_DIM // 2
    first = vectors[:, :half_dim]
    second = vectors[:, half_dim:]
    return jnp.concatenate(
        [first * cosine - second * sine, second * cosine + first * sine], axis=1
    )


def shards(
    token_ids,
    query_order,
    embed_table,
    hyena_gain,
    short_filter,
    decay_rate,
    residue,
    skip_gain,
    attn_gain,
    w_qkv,
):
    length = token_ids.shape[0]
    vocab = embed_table.shape[0]
    here = embed_table.shape[1]
    span = min(SPAN_MOST, here)
    spans = here // span
    tiles = span // 128
    nctx = lax.axis_size("ctx")
    rank = lax.axis_index("ctx")
    padded = length + HALO
    weights_full = lax.all_gather(w_qkv, "ctx", axis=0, tiled=True)
    earlier_ids = lax.ppermute(
        token_ids[length - HALO :], "ctx", [(i, i + 1) for i in range(nctx - 1)]
    )
    ids = jnp.concatenate([earlier_ids, token_ids])
    table_wide = embed_table.astype(jnp.float32)
    (table_parts,) = gather_direct(
        "ch", [packed(jnp.sum(table_wide * table_wide, axis=1))], (False,), 1
    )
    table_energy = jnp.sum(table_parts, axis=0).reshape(-1)[:vocab]
    energy = jnp.sum(
        jnp.where(
            ids[:, None] == jnp.arange(vocab, dtype=jnp.int32)[None, :], table_energy[None, :], 0.0
        ),
        axis=1,
    )
    real = (jnp.arange(padded) >= HALO) | (rank > 0)
    scale = jnp.where(real, lax.rsqrt(energy / D + 1e-06), 0.0)
    decay_tiles = decay_rate.reshape(ORDER, spans, tiles, 128).swapaxes(0, 1)
    residue_tiles = residue.reshape(ORDER, spans, tiles, 128).swapaxes(0, 1)
    row = lambda size: pl.BlockSpec((size, span), lambda h: (0, h))
    tile = pl.BlockSpec((None, ORDER, tiles, 128), lambda h: (h, 0, 0, 0))
    lone = lambda size: pl.BlockSpec((size, 1), lambda h: (0, 0))
    local = pl.pallas_call(
        modal_local,
        grid=(spans,),
        in_specs=[
            lone(padded), lone(padded), row(vocab), row(1), row(9), tile, tile, row(1)
        ],
        out_specs=[row(length), row(length), tile],
        out_shape=[
            jax.ShapeDtypeStruct((length, here), jnp.float32),
            jax.ShapeDtypeStruct((length, here), jnp.float32),
            jax.ShapeDtypeStruct((spans, ORDER, tiles, 128), jnp.float32),
        ],
        scratch_shapes=[
            pltpu.VMEM((padded, span), jnp.float32),
            pltpu.VMEM((length * tiles, 128), jnp.float32),
            pltpu.VMEM((length * tiles, 128), jnp.float32),
        ],
        name="modal_local",
    )
    local_args = (
        ids[:, None],
        scale[:, None],
        embed_table,
        hyena_gain[None],
        short_filter.reshape(9, here),
        decay_tiles,
        residue_tiles,
        skip_gain[None],
    )
    query, base, state = local(*local_args)
    states = gather_paired(
        "ctx", state.reshape(spans * ORDER * tiles, 128), 2
    ).reshape(nctx, spans, ORDER, tiles, 128)
    mixed, scaled, lanes = pl.pallas_call(
        modal_finish,
        grid_spec=pltpu.PrefetchScalarGridSpec(
            num_scalar_prefetch=1,
            grid=(spans,),
            in_specs=[
                pl.BlockSpec((nctx, None, ORDER, tiles, 128), lambda h, s: (0, h, 0, 0, 0)),
                pl.BlockSpec((None, ORDER, tiles, 128), lambda h, s: (h, 0, 0, 0)),
                pl.BlockSpec((None, ORDER, tiles, 128), lambda h, s: (h, 0, 0, 0)),
                pl.BlockSpec((length, span), lambda h, s: (0, h)),
                pl.BlockSpec((length, span), lambda h, s: (0, h)),
                pl.BlockSpec((1, span), lambda h, s: (0, h)),
            ],
            out_specs=[
                pl.BlockSpec((length, span), lambda h, s: (0, h)),
                pl.BlockSpec((length, span), lambda h, s: (0, h)),
                pl.BlockSpec((length, 128), lambda h, s: (0, 0)),
            ],
            scratch_shapes=[pltpu.VMEM((length * tiles, 128), jnp.float32)],
        ),
        out_shape=[
            jax.ShapeDtypeStruct((length, here), jnp.bfloat16),
            jax.ShapeDtypeStruct((length, here), jnp.bfloat16),
            jax.ShapeDtypeStruct((length, 128), jnp.float32),
        ],
        name="modal_finish",
    )(rank[None], states, decay_tiles, residue_tiles, query, base, attn_gain[None])
    scaled_full, energy_parts = gather_direct(
        "ch", [scaled, packed(jnp.sum(lanes, axis=1))], (True, False), 3
    )
    stream_energy = jnp.sum(energy_parts, axis=0).reshape(-1)[:length]
    row_scale = lax.rsqrt(stream_energy / D + 1e-06)[:, None]
    projected = (
        jnp.dot(scaled_full, weights_full, preferred_element_type=jnp.float32) * row_scale
    )
    half_dim = HEAD_DIM // 2
    positions = rank * length + jnp.arange(length, dtype=jnp.int32)
    frequency = 10000.0 ** (-(jnp.arange(half_dim, dtype=jnp.float32) / half_dim))
    angle = positions.astype(jnp.float32)[:, None] * frequency[None, :]
    cosine, sine = jnp.cos(angle), jnp.sin(angle)
    width = HEAD_DIM
    qkv = jnp.concatenate(
        [
            rotate(projected[:, :width], cosine, sine),
            rotate(projected[:, width : 2 * width], cosine, sine),
            projected[:, 2 * width :],
        ],
        axis=1,
    ).astype(jnp.bfloat16)
    every = gather_paired("ctx", qkv, 4).reshape(nctx * length, 3 * width)
    blocks = lax.dynamic_slice_in_dim(query_order, rank * 2, 2)
    attended = pl.pallas_call(
        attend,
        in_specs=[
            pl.BlockSpec(memory_space=pltpu.SMEM),
            pl.BlockSpec(memory_space=pltpu.VMEM),
        ],
        out_specs=pl.BlockSpec(memory_space=pltpu.VMEM),
        out_shape=jax.ShapeDtypeStruct((length, width), jnp.bfloat16),
        name="attend",
    )(blocks, every)
    return (mixed, attended)


def solution(mesh):
    placed = (
        P("ctx"),
        P(),
        P(None, "ch"),
        P("ch"),
        P(None, None, "ch"),
        P(None, "ch"),
        P(None, "ch"),
        P("ch"),
        P("ch"),
        P("ctx", "ch"),
    )
    return jax.shard_map(
        shards,
        mesh=mesh,
        in_specs=placed,
        out_specs=(P("ctx", "ch"), P("ctx", "ch")),
        check_vma=False,
    )
```

```python
import functools
import math

import jax
import jax.numpy as jnp
from jax import lax
from jax.experimental import pallas as pl
from jax.experimental.pallas import tpu as pltpu
from jax.sharding import PartitionSpec as P

D = 8192
HEAD_DIM = 128
SHORT = 3
ORDER = 16
HALO = 16
SPAN_MOST = 1024


def modal_local(
    ids_ref,
    scale_ref,
    table_ref,
    gain_ref,
    taps_ref,
    decay_ref,
    residue_ref,
    skip_ref,
    query_ref,
    base_ref,
    state_ref,
    normed_ref,
    gated_ref,
    long_ref,
):
    rows = query_ref.shape[0]
    vocab, span = table_ref.shape
    tiles = span // 128
    padded = ids_ref.shape[0]
    onehot = (
        (ids_ref[...] == lax.broadcasted_iota(jnp.int32, (padded, vocab), 1))
        .astype(jnp.float32)
        .astype(jnp.bfloat16)
    )
    embedded = jnp.dot(onehot, table_ref[...], preferred_element_type=jnp.float32)
    base_ref[...] = embedded[HALO:]
    normed_ref[...] = (
        (embedded * scale_ref[...] * gain_ref[...]).astype(jnp.bfloat16).astype(jnp.float32)
    )
    taps = taps_ref[...]

    def stream(j):
        total = taps[3 * j : 3 * j + 1] * normed_ref[HALO:]
        for i in range(1, SHORT):
            k = 3 * j + i
            total = total + taps[k : k + 1] * normed_ref[HALO - i : HALO - i + rows]
        return total

    query = stream(0)
    gated = stream(1) * stream(2)
    query_ref[...] = query
    base_ref[...] += query * (skip_ref[...] * gated)
    for r in range(rows // 8):
        for k in range(tiles):
            gated_ref[(r * tiles + k) * 8 : (r * tiles + k + 1) * 8, :] = gated[
                r * 8 : r * 8 + 8, k * 128 : k * 128 + 128
            ]
    decay = [jnp.exp(-decay_ref[n]) for n in range(ORDER)]

    def step(r, states):
        states = list(states)
        for t in range(8):
            place = pl.ds(r * (8 * tiles) + t, tiles, stride=8)
            entry = gated_ref[place, :]
            terms = []
            for n in range(ORDER):
                states[n] = decay[n] * states[n] + entry
                terms.append(residue_ref[n] * states[n])
            while len(terms) > 1:
                terms = [a + b for a, b in zip(terms[::2], terms[1::2])]
            long_ref[place, :] = terms[0]
        return tuple(states)

    zero = jnp.zeros((tiles, 128), jnp.float32)
    states = lax.fori_loop(0, rows // 8, step, (zero,) * ORDER)
    for n in range(ORDER):
        state_ref[n] = states[n].astype(state_ref.dtype)
    for r in range(rows // 8):
        for k in range(tiles):
            spot = (slice(r * 8, r * 8 + 8), slice(k * 128, k * 128 + 128))
            base_ref[spot] += (
                query_ref[spot] * long_ref[(r * tiles + k) * 8 : (r * tiles + k + 1) * 8, :]
            )


def modal_finish(
    rank_ref,
    states_ref,
    decay_ref,
    residue_ref,
    query_ref,
    base_ref,
    gain_ref,
    mixed_ref,
    scaled_ref,
    energy_ref,
    long_ref,
):
    rows, span = query_ref.shape
    tiles = span // 128
    rank = rank_ref[0]
    block_decay = [jnp.exp(-decay_ref[n] * float(rows)) for n in range(ORDER)]

    def carry(k, states):
        return tuple(states[n] * block_decay[n] + states_ref[k, n].astype(jnp.float32) for n in range(ORDER))

    zero = jnp.zeros((tiles, 128), jnp.float32)
    incoming = lax.fori_loop(0, rank, carry, (zero,) * ORDER)
    decay = [jnp.exp(-decay_ref[n]) for n in range(ORDER)]

    def step(r, terms):
        terms = list(terms)
        for t in range(8):
            terms = [decay[n] * terms[n] for n in range(ORDER)]
            sums = terms
            while len(sums) > 1:
                sums = [a + b for a, b in zip(sums[::2], sums[1::2])]
            long_ref[pl.ds(r * (8 * tiles) + t, tiles, stride=8), :] = sums[0]
        return tuple(terms)

    lax.fori_loop(
        0, rows // 8, step, tuple(residue_ref[n] * incoming[n] for n in range(ORDER))
    )

    @pl.when(pl.program_id(0) == 0)
    def _():
        energy_ref[...] = jnp.zeros_like(energy_ref)

    for r in range(rows // 16):
        energy = jnp.zeros((16, 128), jnp.float32)
        for k in range(tiles):
            spot = (slice(r * 16, r * 16 + 16), slice(k * 128, k * 128 + 128))
            first = (2 * r * tiles + k) * 8
            second = ((2 * r + 1) * tiles + k) * 8
            late = jnp.concatenate(
                [long_ref[first : first + 8, :], long_ref[second : second + 8, :]], axis=0
            )
            mixed = (base_ref[spot] + query_ref[spot] * late).astype(jnp.bfloat16)
            mixed_ref[spot] = mixed
            wide = mixed.astype(jnp.float32)
            scaled_ref[spot] = (wide * gain_ref[:, spot[1]]).astype(jnp.bfloat16)
            energy = energy + wide * wide
        energy_ref[r * 16 : r * 16 + 16, :] += energy


def direct_kernel(axis, columns, count, *refs):
    ins, outs = refs[:count], refs[count : 2 * count]
    send, recv, own = refs[2 * count :]
    size, me = lax.axis_size(axis), lax.axis_index(axis)
    barrier = pltpu.get_barrier_semaphore()
    for d in range(1, size):
        peer = lax.rem(me + d, size)
        pl.semaphore_signal(
            barrier, inc=1, device_id={axis: peer}, device_id_type=pl.DeviceIdType.MESH
        )
    pl.semaphore_wait(barrier, size - 1)
    copies = []
    for a in range(count):
        if columns[a]:
            width = ins[a].shape[1]
            spot = outs[a].at[:, pl.ds(pl.multiple_of(me * width, 128), width)]
        else:
            spot = outs[a].at[me]
        for d in range(1, size):
            copies.append(
                pltpu.make_async_remote_copy(
                    src_ref=ins[a],
                    dst_ref=spot,
                    send_sem=send.at[a, d - 1],
                    recv_sem=recv.at[a, d - 1],
                    device_id={axis: lax.rem(me + d, size)},
                    device_id_type=pl.DeviceIdType.MESH,
                )
            )
        copies.append(pltpu.make_async_copy(ins[a], spot, own.at[a]))
    for copy in copies:
        copy.start()
    for copy in copies:
        copy.wait()


def square_kernel(
    axis, in_ref, small_ref, out_ref, small_out_ref, send, recv, small_send, small_recv, own
):
    me = lax.axis_index(axis)
    y, x = lax.div(me, 2), lax.rem(me, 2)
    beside, above = y * 2 + 1 - x, (1 - y) * 2 + x
    peers = [beside, above, (1 - y) * 2 + 1 - x]
    barrier = pltpu.get_barrier_semaphore()
    for peer in peers:
        pl.semaphore_signal(
            barrier, inc=1, device_id={axis: peer}, device_id_type=pl.DeviceIdType.MESH
        )
    pl.semaphore_wait(barrier, 3)
    rows, width = in_ref.shape
    half = rows // 2

    def spot(owner, part):
        return out_ref.at[
            part * half : (part + 1) * half, pl.ds(pl.multiple_of(owner * width, 128), width)
        ]

    def remote(source, target, slot, peer):
        return pltpu.make_async_remote_copy(
            src_ref=source,
            dst_ref=target,
            send_sem=send.at[slot],
            recv_sem=recv.at[slot],
            device_id={axis: peer},
            device_id_type=pl.DeviceIdType.MESH,
        )

    parts = [in_ref.at[:half], in_ref.at[half:]]
    first = remote(parts[0], spot(me, 0), 0, beside)
    second = remote(parts[1], spot(me, 1), 1, above)
    third = remote(parts[1], spot(me, 1), 2, beside)
    fourth = remote(parts[0], spot(me, 0), 3, above)
    small = [
        pltpu.make_async_remote_copy(
            src_ref=small_ref,
            dst_ref=small_out_ref.at[me],
            send_sem=small_send.at[d],
            recv_sem=small_recv.at[d],
            device_id={axis: peers[d]},
            device_id_type=pl.DeviceIdType.MESH,
        )
        for d in range(3)
    ]
    mine = [
        pltpu.make_async_copy(parts[0], spot(me, 0), own.at[0]),
        pltpu.make_async_copy(parts[1], spot(me, 1), own.at[1]),
        pltpu.make_async_copy(small_ref, small_out_ref.at[me], own.at[2]),
    ]
    for copy in [first, second] + small + [third, fourth] + mine:
        copy.start()
    first.wait_recv()
    onward = remote(spot(beside, 0), spot(beside, 0), 4, above)
    onward.start()
    second.wait_recv()
    across = remote(spot(above, 1), spot(above, 1), 5, beside)
    across.start()
    first.wait_send()
    second.wait_send()
    for copy in [third, fourth] + small + mine + [onward, across]:
        copy.wait()


def paired_kernel(axis, in_ref, out_ref, send, recv, hand_send, hand_recv, own):
    size, me = lax.axis_size(axis), lax.axis_index(axis)
    chips = size // 2
    chip, core = lax.div(me, 2), lax.rem(me, 2)
    sibling = me + 1 - 2 * core
    peers = [sibling] + [lax.rem(chip + d, chips) * 2 + core for d in range(1, chips)]
    barrier = pltpu.get_barrier_semaphore()
    for peer in peers:
        pl.semaphore_signal(
            barrier, inc=1, device_id={axis: peer}, device_id_type=pl.DeviceIdType.MESH
        )
    pl.semaphore_wait(barrier, chips)
    copies = [
        pltpu.make_async_remote_copy(
            src_ref=in_ref,
            dst_ref=out_ref.at[me],
            send_sem=send.at[d],
            recv_sem=recv.at[d],
            device_id={axis: peers[d]},
            device_id_type=pl.DeviceIdType.MESH,
        )
        for d in range(chips)
    ]
    for copy in copies[1:]:
        copy.start()
    copies[0].start()
    mine = pltpu.make_async_copy(in_ref, out_ref.at[me], own)
    mine.start()
    hands = []
    for d in range(1, chips):
        copies[d].wait_recv()
        source = lax.rem(chip + chips - d, chips) * 2 + core
        hand = pltpu.make_async_remote_copy(
            src_ref=out_ref.at[source],
            dst_ref=out_ref.at[source],
            send_sem=hand_send.at[d],
            recv_sem=hand_recv.at[d],
            device_id={axis: sibling},
            device_id_type=pl.DeviceIdType.MESH,
        )
        hand.start()
        hands.append(hand)
    mine.wait()
    copies[0].wait_recv()
    for copy in copies:
        copy.wait_send()
    for hand in hands:
        hand.wait()


def gather_direct(axis, arrays, columns, collective_id):
    size, count = lax.axis_size(axis), len(arrays)
    vmem = pl.BlockSpec(memory_space=pltpu.VMEM)
    dma = pltpu.SemaphoreType.DMA
    return pl.pallas_call(
        functools.partial(direct_kernel, axis, columns, count),
        in_specs=[vmem] * count,
        out_specs=[vmem] * count,
        out_shape=[
            jax.ShapeDtypeStruct(
                (a.shape[0], size * a.shape[1]) if wide else (size,) + a.shape, a.dtype
            )
            for a, wide in zip(arrays, columns)
        ],
        scratch_shapes=[dma((count, size - 1)), dma((count, size - 1)), dma((count,))],
        compiler_params=pltpu.CompilerParams(
            collective_id=collective_id, has_side_effects=True
        ),
    )(*arrays)


def gather_square(axis, array, small, collective_id):
    size = lax.axis_size(axis)
    if size != 4:
        return gather_direct(axis, [array, small], (True, False), collective_id)
    vmem = pl.BlockSpec(memory_space=pltpu.VMEM)
    dma = pltpu.SemaphoreType.DMA
    return pl.pallas_call(
        functools.partial(square_kernel, axis),
        in_specs=[vmem, vmem],
        out_specs=[vmem, vmem],
        out_shape=[
            jax.ShapeDtypeStruct((array.shape[0], size * array.shape[1]), array.dtype),
            jax.ShapeDtypeStruct((size,) + small.shape, small.dtype),
        ],
        scratch_shapes=[dma((6,)), dma((6,)), dma((3,)), dma((3,)), dma((3,))],
        compiler_params=pltpu.CompilerParams(
            collective_id=collective_id, has_side_effects=True
        ),
    )(array, small)


def gather_paired(axis, array, collective_id):
    size = lax.axis_size(axis)
    vmem = pl.BlockSpec(memory_space=pltpu.VMEM)
    dma = pltpu.SemaphoreType.DMA
    chips = size // 2
    return pl.pallas_call(
        functools.partial(paired_kernel, axis),
        in_specs=[vmem],
        out_specs=vmem,
        out_shape=jax.ShapeDtypeStruct((size,) + array.shape, array.dtype),
        scratch_shapes=[dma((chips,)), dma((chips,)), dma((chips,)), dma((chips,)), dma(())],
        compiler_params=pltpu.CompilerParams(
            collective_id=collective_id, has_side_effects=True
        ),
    )(array)


def packed(vector):
    wide = -(-vector.shape[0] // 1024) * 1024
    return jnp.pad(vector, (0, wide - vector.shape[0])).reshape(wide // 128, 128)


def attend(blocks_ref, qkv_ref, out_ref):
    half_rows = out_ref.shape[0] // 2
    keys_total = qkv_ref.shape[0]
    width = HEAD_DIM
    for b in range(2):
        start = pl.multiple_of(blocks_ref[b] * half_rows, 32)
        queries = qkv_ref[pl.ds(start, half_rows), :width]
        keys = qkv_ref[:, width : 2 * width]
        values = qkv_ref[:, 2 * width :]
        scores = lax.dot_general(
            queries, keys, (((1,), (1,)), ((), ())), preferred_element_type=jnp.float32
        ) * (1.0 / math.sqrt(HEAD_DIM))
        at = start + lax.broadcasted_iota(jnp.int32, (half_rows, keys_total), 0)
        allowed = lax.broadcasted_iota(jnp.int32, (half_rows, keys_total), 1) <= at
        masked = jnp.where(allowed, scores, -1e30)
        top = jnp.max(masked, axis=1, keepdims=True)
        weights = jnp.where(allowed, jnp.exp(masked - top), 0.0)
        total = jnp.sum(weights, axis=1, keepdims=True)
        out = jnp.dot(weights.astype(jnp.bfloat16), values, preferred_element_type=jnp.float32)
        out_ref[b * half_rows : (b + 1) * half_rows, :] = (out / total).astype(jnp.bfloat16)


def rotate(vectors, cosine, sine):
    half_dim = HEAD_DIM // 2
    first = vectors[:, :half_dim]
    second = vectors[:, half_dim:]
    return jnp.concatenate(
        [first * cosine - second * sine, second * cosine + first * sine], axis=1
    )


def shards(
    token_ids,
    query_order,
    embed_table,
    hyena_gain,
    short_filter,
    decay_rate,
    residue,
    skip_gain,
    attn_gain,
    w_qkv,
):
    length = token_ids.shape[0]
    vocab = embed_table.shape[0]
    here = embed_table.shape[1]
    span = min(SPAN_MOST, here)
    spans = here // span
    tiles = span // 128
    nctx = lax.axis_size("ctx")
    rank = lax.axis_index("ctx")
    padded = length + HALO
    weights_full = lax.all_gather(w_qkv, "ctx", axis=0, tiled=True)
    earlier_ids = lax.ppermute(
        token_ids[length - HALO :], "ctx", [(i, i + 1) for i in range(nctx - 1)]
    )
    ids = jnp.concatenate([earlier_ids, token_ids])
    table_wide = embed_table.astype(jnp.float32)
    (table_parts,) = gather_direct(
        "ch", [packed(jnp.sum(table_wide * table_wide, axis=1))], (False,), 1
    )
    table_energy = jnp.sum(table_parts, axis=0).reshape(-1)[:vocab]
    energy = jnp.sum(
        jnp.where(
            ids[:, None] == jnp.arange(vocab, dtype=jnp.int32)[None, :], table_energy[None, :], 0.0
        ),
        axis=1,
    )
    real = (jnp.arange(padded) >= HALO) | (rank > 0)
    scale = jnp.where(real, lax.rsqrt(energy / D + 1e-06), 0.0)
    decay_tiles = decay_rate.reshape(ORDER, spans, tiles, 128).swapaxes(0, 1)
    residue_tiles = residue.reshape(ORDER, spans, tiles, 128).swapaxes(0, 1)
    row = lambda size: pl.BlockSpec((size, span), lambda h: (0, h))
    tile = pl.BlockSpec((None, ORDER, tiles, 128), lambda h: (h, 0, 0, 0))
    lone = lambda size: pl.BlockSpec((size, 1), lambda h: (0, 0))
    local = pl.pallas_call(
        modal_local,
        grid=(spans,),
        in_specs=[
            lone(padded), lone(padded), row(vocab), row(1), row(9), tile, tile, row(1)
        ],
        out_specs=[row(length), row(length), tile],
        out_shape=[
            jax.ShapeDtypeStruct((length, here), jnp.float32),
            jax.ShapeDtypeStruct((length, here), jnp.float32),
            jax.ShapeDtypeStruct((spans, ORDER, tiles, 128), jnp.bfloat16),
        ],
        scratch_shapes=[
            pltpu.VMEM((padded, span), jnp.float32),
            pltpu.VMEM((length * tiles, 128), jnp.float32),
            pltpu.VMEM((length * tiles, 128), jnp.float32),
        ],
        name="modal_local",
    )
    local_args = (
        ids[:, None],
        scale[:, None],
        embed_table,
        hyena_gain[None],
        short_filter.reshape(9, here),
        decay_tiles,
        residue_tiles,
        skip_gain[None],
    )
    query, base, state = local(*local_args)
    states = gather_paired(
        "ctx", state.reshape(spans * ORDER * tiles, 128), 2
    ).reshape(nctx, spans, ORDER, tiles, 128)
    mixed, scaled, lanes = pl.pallas_call(
        modal_finish,
        grid_spec=pltpu.PrefetchScalarGridSpec(
            num_scalar_prefetch=1,
            grid=(spans,),
            in_specs=[
                pl.BlockSpec((nctx, None, ORDER, tiles, 128), lambda h, s: (0, h, 0, 0, 0)),
                pl.BlockSpec((None, ORDER, tiles, 128), lambda h, s: (h, 0, 0, 0)),
                pl.BlockSpec((None, ORDER, tiles, 128), lambda h, s: (h, 0, 0, 0)),
                pl.BlockSpec((length, span), lambda h, s: (0, h)),
                pl.BlockSpec((length, span), lambda h, s: (0, h)),
                pl.BlockSpec((1, span), lambda h, s: (0, h)),
            ],
            out_specs=[
                pl.BlockSpec((length, span), lambda h, s: (0, h)),
                pl.BlockSpec((length, span), lambda h, s: (0, h)),
                pl.BlockSpec((length, 128), lambda h, s: (0, 0)),
            ],
            scratch_shapes=[pltpu.VMEM((length * tiles, 128), jnp.float32)],
        ),
        out_shape=[
            jax.ShapeDtypeStruct((length, here), jnp.bfloat16),
            jax.ShapeDtypeStruct((length, here), jnp.bfloat16),
            jax.ShapeDtypeStruct((length, 128), jnp.float32),
        ],
        name="modal_finish",
    )(rank[None], states, decay_tiles, residue_tiles, query, base, attn_gain[None])
    scaled_full, energy_parts = gather_square("ch", scaled, packed(jnp.sum(lanes, axis=1)), 3)
    stream_energy = jnp.sum(energy_parts, axis=0).reshape(-1)[:length]
    row_scale = lax.rsqrt(stream_energy / D + 1e-06)[:, None]
    projected = (
        jnp.dot(scaled_full, weights_full, preferred_element_type=jnp.float32) * row_scale
    )
    half_dim = HEAD_DIM // 2
    positions = rank * length + jnp.arange(length, dtype=jnp.int32)
    frequency = 10000.0 ** (-(jnp.arange(half_dim, dtype=jnp.float32) / half_dim))
    angle = positions.astype(jnp.float32)[:, None] * frequency[None, :]
    cosine, sine = jnp.cos(angle), jnp.sin(angle)
    width = HEAD_DIM
    qkv = jnp.concatenate(
        [
            rotate(projected[:, :width], cosine, sine),
            rotate(projected[:, width : 2 * width], cosine, sine),
            projected[:, 2 * width :],
        ],
        axis=1,
    ).astype(jnp.bfloat16)
    every = gather_paired("ctx", qkv, 4).reshape(nctx * length, 3 * width)
    blocks = lax.dynamic_slice_in_dim(query_order, rank * 2, 2)
    attended = pl.pallas_call(
        attend,
        in_specs=[
            pl.BlockSpec(memory_space=pltpu.SMEM),
            pl.BlockSpec(memory_space=pltpu.VMEM),
        ],
        out_specs=pl.BlockSpec(memory_space=pltpu.VMEM),
        out_shape=jax.ShapeDtypeStruct((length, width), jnp.bfloat16),
        name="attend",
    )(blocks, every)
    return (mixed, attended)


def solution(mesh):
    placed = (
        P("ctx"),
        P(),
        P(None, "ch"),
        P("ch"),
        P(None, None, "ch"),
        P(None, "ch"),
        P(None, "ch"),
        P("ch"),
        P("ch"),
        P("ctx", "ch"),
    )
    return jax.shard_map(
        shards,
        mesh=mesh,
        in_specs=placed,
        out_specs=(P("ctx", "ch"), P("ctx", "ch")),
        check_vma=False,
    )
```

```python
import functools
import math

import jax
import jax.numpy as jnp
from jax import lax
from jax.experimental import pallas as pl
from jax.experimental.pallas import tpu as pltpu
from jax.sharding import PartitionSpec as P

D = 8192
HEAD_DIM = 128
SHORT = 3
ORDER = 16
HALO = 16
SPAN_MOST = 1024


def modal_local(
    ids_ref,
    scale_ref,
    table_ref,
    gain_ref,
    taps_ref,
    decay_ref,
    residue_ref,
    skip_ref,
    query_ref,
    base_ref,
    state_ref,
    normed_ref,
    gated_ref,
    long_ref,
):
    rows = query_ref.shape[0]
    vocab, span = table_ref.shape
    tiles = span // 128
    padded = ids_ref.shape[0]
    onehot = (
        (ids_ref[...] == lax.broadcasted_iota(jnp.int32, (padded, vocab), 1))
        .astype(jnp.float32)
        .astype(jnp.bfloat16)
    )
    embedded = jnp.dot(onehot, table_ref[...], preferred_element_type=jnp.float32)
    base_ref[...] = embedded[HALO:]
    normed_ref[...] = (
        (embedded * scale_ref[...] * gain_ref[...]).astype(jnp.bfloat16).astype(jnp.float32)
    )
    taps = taps_ref[...]

    def stream(j):
        total = taps[3 * j : 3 * j + 1] * normed_ref[HALO:]
        for i in range(1, SHORT):
            k = 3 * j + i
            total = total + taps[k : k + 1] * normed_ref[HALO - i : HALO - i + rows]
        return total

    query = stream(0)
    gated = stream(1) * stream(2)
    query_ref[...] = query
    base_ref[...] += query * (skip_ref[...] * gated)
    for r in range(rows // 8):
        for k in range(tiles):
            gated_ref[(r * tiles + k) * 8 : (r * tiles + k + 1) * 8, :] = gated[
                r * 8 : r * 8 + 8, k * 128 : k * 128 + 128
            ]
    decay = [jnp.exp(-decay_ref[n]) for n in range(ORDER)]

    def step(r, states):
        states = list(states)
        for t in range(8):
            place = pl.ds(r * (8 * tiles) + t, tiles, stride=8)
            entry = gated_ref[place, :]
            terms = []
            for n in range(ORDER):
                states[n] = decay[n] * states[n] + entry
                terms.append(residue_ref[n] * states[n])
            while len(terms) > 1:
                terms = [a + b for a, b in zip(terms[::2], terms[1::2])]
            long_ref[place, :] = terms[0]
        return tuple(states)

    zero = jnp.zeros((tiles, 128), jnp.float32)
    states = lax.fori_loop(0, rows // 8, step, (zero,) * ORDER)
    for n in range(ORDER):
        state_ref[n] = states[n].astype(state_ref.dtype)
    for r in range(rows // 8):
        for k in range(tiles):
            spot = (slice(r * 8, r * 8 + 8), slice(k * 128, k * 128 + 128))
            base_ref[spot] += (
                query_ref[spot] * long_ref[(r * tiles + k) * 8 : (r * tiles + k + 1) * 8, :]
            )


def modal_finish(
    rank_ref,
    states_ref,
    decay_ref,
    residue_ref,
    query_ref,
    base_ref,
    gain_ref,
    mixed_ref,
    scaled_ref,
    energy_ref,
    long_ref,
):
    rows, span = query_ref.shape
    tiles = span // 128
    rank = rank_ref[0]
    block_decay = [jnp.exp(-decay_ref[n] * float(rows)) for n in range(ORDER)]

    def carry(k, states):
        return tuple(states[n] * block_decay[n] + states_ref[k, n].astype(jnp.float32) for n in range(ORDER))

    zero = jnp.zeros((tiles, 128), jnp.float32)
    incoming = lax.fori_loop(0, rank, carry, (zero,) * ORDER)
    decay = [jnp.exp(-decay_ref[n]) for n in range(ORDER)]

    def step(r, terms):
        terms = list(terms)
        for t in range(8):
            terms = [decay[n] * terms[n] for n in range(ORDER)]
            sums = terms
            while len(sums) > 1:
                sums = [a + b for a, b in zip(sums[::2], sums[1::2])]
            long_ref[pl.ds(r * (8 * tiles) + t, tiles, stride=8), :] = sums[0]
        return tuple(terms)

    lax.fori_loop(
        0, rows // 8, step, tuple(residue_ref[n] * incoming[n] for n in range(ORDER))
    )

    @pl.when(pl.program_id(0) == 0)
    def _():
        energy_ref[...] = jnp.zeros_like(energy_ref)

    for r in range(rows // 16):
        energy = jnp.zeros((16, 128), jnp.float32)
        for k in range(tiles):
            spot = (slice(r * 16, r * 16 + 16), slice(k * 128, k * 128 + 128))
            first = (2 * r * tiles + k) * 8
            second = ((2 * r + 1) * tiles + k) * 8
            late = jnp.concatenate(
                [long_ref[first : first + 8, :], long_ref[second : second + 8, :]], axis=0
            )
            mixed = (base_ref[spot] + query_ref[spot] * late).astype(jnp.bfloat16)
            mixed_ref[spot] = mixed
            wide = mixed.astype(jnp.float32)
            scaled_ref[spot] = (wide * gain_ref[:, spot[1]]).astype(jnp.bfloat16)
            energy = energy + wide * wide
        energy_ref[r * 16 : r * 16 + 16, :] += energy


def direct_kernel(axis, columns, count, *refs):
    ins, outs = refs[:count], refs[count : 2 * count]
    send, recv, own = refs[2 * count :]
    size, me = lax.axis_size(axis), lax.axis_index(axis)
    barrier = pltpu.get_barrier_semaphore()
    for d in range(1, size):
        peer = lax.rem(me + d, size)
        pl.semaphore_signal(
            barrier, inc=1, device_id={axis: peer}, device_id_type=pl.DeviceIdType.MESH
        )
    pl.semaphore_wait(barrier, size - 1)
    copies = []
    for a in range(count):
        if columns[a]:
            width = ins[a].shape[1]
            spot = outs[a].at[:, pl.ds(pl.multiple_of(me * width, 128), width)]
        else:
            spot = outs[a].at[me]
        for d in range(1, size):
            copies.append(
                pltpu.make_async_remote_copy(
                    src_ref=ins[a],
                    dst_ref=spot,
                    send_sem=send.at[a, d - 1],
                    recv_sem=recv.at[a, d - 1],
                    device_id={axis: lax.rem(me + d, size)},
                    device_id_type=pl.DeviceIdType.MESH,
                )
            )
        copies.append(pltpu.make_async_copy(ins[a], spot, own.at[a]))
    for copy in copies:
        copy.start()
    for copy in copies:
        copy.wait()


def square_kernel(
    axis, in_ref, small_ref, out_ref, small_out_ref, send, recv, small_send, small_recv, own
):
    me = lax.axis_index(axis)
    y, x = lax.div(me, 2), lax.rem(me, 2)
    beside, above = y * 2 + 1 - x, (1 - y) * 2 + x
    peers = [beside, above, (1 - y) * 2 + 1 - x]
    barrier = pltpu.get_barrier_semaphore()
    for peer in peers:
        pl.semaphore_signal(
            barrier, inc=1, device_id={axis: peer}, device_id_type=pl.DeviceIdType.MESH
        )
    pl.semaphore_wait(barrier, 3)
    rows, width = in_ref.shape
    half = rows // 2

    def spot(owner, part):
        return out_ref.at[
            part * half : (part + 1) * half, pl.ds(pl.multiple_of(owner * width, 128), width)
        ]

    def remote(source, target, slot, peer):
        return pltpu.make_async_remote_copy(
            src_ref=source,
            dst_ref=target,
            send_sem=send.at[slot],
            recv_sem=recv.at[slot],
            device_id={axis: peer},
            device_id_type=pl.DeviceIdType.MESH,
        )

    parts = [in_ref.at[:half], in_ref.at[half:]]
    first = remote(parts[0], spot(me, 0), 0, beside)
    second = remote(parts[1], spot(me, 1), 1, above)
    third = remote(parts[1], spot(me, 1), 2, beside)
    fourth = remote(parts[0], spot(me, 0), 3, above)
    small = [
        pltpu.make_async_remote_copy(
            src_ref=small_ref,
            dst_ref=small_out_ref.at[me],
            send_sem=small_send.at[d],
            recv_sem=small_recv.at[d],
            device_id={axis: peers[d]},
            device_id_type=pl.DeviceIdType.MESH,
        )
        for d in range(3)
    ]
    mine = [
        pltpu.make_async_copy(parts[0], spot(me, 0), own.at[0]),
        pltpu.make_async_copy(parts[1], spot(me, 1), own.at[1]),
        pltpu.make_async_copy(small_ref, small_out_ref.at[me], own.at[2]),
    ]
    for copy in [first, second] + small + [third, fourth] + mine:
        copy.start()
    first.wait_recv()
    onward = remote(spot(beside, 0), spot(beside, 0), 4, above)
    onward.start()
    second.wait_recv()
    across = remote(spot(above, 1), spot(above, 1), 5, beside)
    across.start()
    first.wait_send()
    second.wait_send()
    for copy in [third, fourth] + small + mine + [onward, across]:
        copy.wait()


def paired_kernel(axis, pieces, in_ref, out_ref, send, recv, hand_send, hand_recv, own):
    size, me = lax.axis_size(axis), lax.axis_index(axis)
    chips = size // 2
    chip, core = lax.div(me, 2), lax.rem(me, 2)
    sibling = me + 1 - 2 * core
    ways = ((1, chip < chips - 1), (-1, chip > 0))
    barrier = pltpu.get_barrier_semaphore()

    def greet(peer):
        pl.semaphore_signal(
            barrier, inc=1, device_id={axis: peer}, device_id_type=pl.DeviceIdType.MESH
        )

    greet(sibling)
    for way, open_ in ways:
        pl.when(open_)(functools.partial(greet, me + 2 * way))
    for count in (2, 3):
        inner = (chip > 0) & (chip < chips - 1)
        pl.when(inner if count == 3 else jnp.logical_not(inner))(
            functools.partial(pl.semaphore_wait, barrier, count)
        )
    rows = in_ref.shape[0] // pieces

    def remote(source, owner, part, sends, recvs, spot, peer):
        return pltpu.make_async_remote_copy(
            src_ref=source,
            dst_ref=out_ref.at[owner, part * rows : (part + 1) * rows],
            send_sem=sends.at[spot],
            recv_sem=recvs.at[spot],
            device_id={axis: peer},
            device_id_type=pl.DeviceIdType.MESH,
        )

    def block(owner, part):
        return out_ref.at[owner, part * rows : (part + 1) * rows]

    def outgoing(w, d, part):
        way = ways[w][0]
        owner = me - 2 * way * (d - 1)
        source = in_ref.at[part * rows : (part + 1) * rows] if d == 1 else block(owner, part)
        return remote(source, owner, part, send, recv, (w, d - 1, part), me + 2 * way)

    def incoming(w, d, part):
        owner = me - 2 * ways[w][0] * d
        return remote(
            block(owner, part), owner, part, send, recv, (w, d - 1, part), sibling
        )

    def handed(w, d, part):
        owner = me - 2 * ways[w][0] * d
        return remote(
            block(owner, part), owner, part, hand_send, hand_recv, (w, d, part), sibling
        )

    def arrives(w, d):
        return chip >= d if w == 0 else chip + d < chips

    for part in range(pieces):
        for w in range(2):
            pl.when(ways[w][1])(lambda w=w, part=part: outgoing(w, 1, part).start())
    for part in range(pieces):
        remote(
            in_ref.at[part * rows : (part + 1) * rows],
            me,
            part,
            hand_send,
            hand_recv,
            (0, 0, part),
            sibling,
        ).start()
    mine = pltpu.make_async_copy(in_ref, out_ref.at[me], own)
    mine.start()

    def relay(w, d, part):
        incoming(w, d, part).wait_recv()
        if d < chips - 1:
            pl.when(ways[w][1])(lambda: outgoing(w, d + 1, part).start())
        handed(w, d, part).start()

    for d in range(1, chips):
        for part in range(pieces):
            for w in range(2):
                pl.when(arrives(w, d))(functools.partial(relay, w, d, part))
    mine.wait()
    for part in range(pieces):
        remote(
            in_ref.at[part * rows : (part + 1) * rows],
            me,
            part,
            hand_send,
            hand_recv,
            (0, 0, part),
            sibling,
        ).wait()
        for w in range(2):
            pl.when(ways[w][1])(lambda w=w, part=part: outgoing(w, 1, part).wait_send())
            for d in range(1, chips):

                def finish(w=w, d=d, part=part):
                    handed(w, d, part).wait()
                    if d < chips - 1:
                        pl.when(ways[w][1])(lambda: outgoing(w, d + 1, part).wait_send())

                pl.when(arrives(w, d))(finish)


def gather_direct(axis, arrays, columns, collective_id):
    size, count = lax.axis_size(axis), len(arrays)
    vmem = pl.BlockSpec(memory_space=pltpu.VMEM)
    dma = pltpu.SemaphoreType.DMA
    return pl.pallas_call(
        functools.partial(direct_kernel, axis, columns, count),
        in_specs=[vmem] * count,
        out_specs=[vmem] * count,
        out_shape=[
            jax.ShapeDtypeStruct(
                (a.shape[0], size * a.shape[1]) if wide else (size,) + a.shape, a.dtype
            )
            for a, wide in zip(arrays, columns)
        ],
        scratch_shapes=[dma((count, size - 1)), dma((count, size - 1)), dma((count,))],
        compiler_params=pltpu.CompilerParams(
            collective_id=collective_id, has_side_effects=True
        ),
    )(*arrays)


def gather_square(axis, array, small, collective_id):
    size = lax.axis_size(axis)
    if size != 4:
        return gather_direct(axis, [array, small], (True, False), collective_id)
    vmem = pl.BlockSpec(memory_space=pltpu.VMEM)
    dma = pltpu.SemaphoreType.DMA
    return pl.pallas_call(
        functools.partial(square_kernel, axis),
        in_specs=[vmem, vmem],
        out_specs=[vmem, vmem],
        out_shape=[
            jax.ShapeDtypeStruct((array.shape[0], size * array.shape[1]), array.dtype),
            jax.ShapeDtypeStruct((size,) + small.shape, small.dtype),
        ],
        scratch_shapes=[dma((6,)), dma((6,)), dma((3,)), dma((3,)), dma((3,))],
        compiler_params=pltpu.CompilerParams(
            collective_id=collective_id, has_side_effects=True
        ),
    )(array, small)


def gather_paired(axis, array, collective_id):
    size = lax.axis_size(axis)
    vmem = pl.BlockSpec(memory_space=pltpu.VMEM)
    dma = pltpu.SemaphoreType.DMA
    chips, pieces = size // 2, 2
    return pl.pallas_call(
        functools.partial(paired_kernel, axis, pieces),
        in_specs=[vmem],
        out_specs=vmem,
        out_shape=jax.ShapeDtypeStruct((size,) + array.shape, array.dtype),
        scratch_shapes=[dma((2, chips, pieces))] * 4 + [dma(())],
        compiler_params=pltpu.CompilerParams(
            collective_id=collective_id, has_side_effects=True
        ),
    )(array)


def packed(vector):
    wide = -(-vector.shape[0] // 1024) * 1024
    return jnp.pad(vector, (0, wide - vector.shape[0])).reshape(wide // 128, 128)


def attend(blocks_ref, qkv_ref, out_ref):
    half_rows = out_ref.shape[0] // 2
    keys_total = qkv_ref.shape[0]
    width = HEAD_DIM
    for b in range(2):
        start = pl.multiple_of(blocks_ref[b] * half_rows, 32)
        queries = qkv_ref[pl.ds(start, half_rows), :width]
        keys = qkv_ref[:, width : 2 * width]
        values = qkv_ref[:, 2 * width :]
        scores = lax.dot_general(
            queries, keys, (((1,), (1,)), ((), ())), preferred_element_type=jnp.float32
        ) * (1.0 / math.sqrt(HEAD_DIM))
        at = start + lax.broadcasted_iota(jnp.int32, (half_rows, keys_total), 0)
        allowed = lax.broadcasted_iota(jnp.int32, (half_rows, keys_total), 1) <= at
        masked = jnp.where(allowed, scores, -1e30)
        top = jnp.max(masked, axis=1, keepdims=True)
        weights = jnp.where(allowed, jnp.exp(masked - top), 0.0)
        total = jnp.sum(weights, axis=1, keepdims=True)
        out = jnp.dot(weights.astype(jnp.bfloat16), values, preferred_element_type=jnp.float32)
        out_ref[b * half_rows : (b + 1) * half_rows, :] = (out / total).astype(jnp.bfloat16)


def rotate(vectors, cosine, sine):
    half_dim = HEAD_DIM // 2
    first = vectors[:, :half_dim]
    second = vectors[:, half_dim:]
    return jnp.concatenate(
        [first * cosine - second * sine, second * cosine + first * sine], axis=1
    )


def shards(
    token_ids,
    query_order,
    embed_table,
    hyena_gain,
    short_filter,
    decay_rate,
    residue,
    skip_gain,
    attn_gain,
    w_qkv,
):
    length = token_ids.shape[0]
    vocab = embed_table.shape[0]
    here = embed_table.shape[1]
    span = min(SPAN_MOST, here)
    spans = here // span
    tiles = span // 128
    nctx = lax.axis_size("ctx")
    rank = lax.axis_index("ctx")
    padded = length + HALO
    weights_full = lax.all_gather(w_qkv, "ctx", axis=0, tiled=True)
    earlier_ids = lax.ppermute(
        token_ids[length - HALO :], "ctx", [(i, i + 1) for i in range(nctx - 1)]
    )
    ids = jnp.concatenate([earlier_ids, token_ids])
    table_wide = embed_table.astype(jnp.float32)
    (table_parts,) = gather_direct(
        "ch", [packed(jnp.sum(table_wide * table_wide, axis=1))], (False,), 1
    )
    table_energy = jnp.sum(table_parts, axis=0).reshape(-1)[:vocab]
    energy = jnp.sum(
        jnp.where(
            ids[:, None] == jnp.arange(vocab, dtype=jnp.int32)[None, :], table_energy[None, :], 0.0
        ),
        axis=1,
    )
    real = (jnp.arange(padded) >= HALO) | (rank > 0)
    scale = jnp.where(real, lax.rsqrt(energy / D + 1e-06), 0.0)
    decay_tiles = decay_rate.reshape(ORDER, spans, tiles, 128).swapaxes(0, 1)
    residue_tiles = residue.reshape(ORDER, spans, tiles, 128).swapaxes(0, 1)
    row = lambda size: pl.BlockSpec((size, span), lambda h: (0, h))
    tile = pl.BlockSpec((None, ORDER, tiles, 128), lambda h: (h, 0, 0, 0))
    lone = lambda size: pl.BlockSpec((size, 1), lambda h: (0, 0))
    local = pl.pallas_call(
        modal_local,
        grid=(spans,),
        in_specs=[
            lone(padded), lone(padded), row(vocab), row(1), row(9), tile, tile, row(1)
        ],
        out_specs=[row(length), row(length), tile],
        out_shape=[
            jax.ShapeDtypeStruct((length, here), jnp.float32),
            jax.ShapeDtypeStruct((length, here), jnp.float32),
            jax.ShapeDtypeStruct((spans, ORDER, tiles, 128), jnp.bfloat16),
        ],
        scratch_shapes=[
            pltpu.VMEM((padded, span), jnp.float32),
            pltpu.VMEM((length * tiles, 128), jnp.float32),
            pltpu.VMEM((length * tiles, 128), jnp.float32),
        ],
        name="modal_local",
    )
    local_args = (
        ids[:, None],
        scale[:, None],
        embed_table,
        hyena_gain[None],
        short_filter.reshape(9, here),
        decay_tiles,
        residue_tiles,
        skip_gain[None],
    )
    query, base, state = local(*local_args)
    states = gather_paired(
        "ctx", state.reshape(spans * ORDER * tiles, 128), 2
    ).reshape(nctx, spans, ORDER, tiles, 128)
    mixed, scaled, lanes = pl.pallas_call(
        modal_finish,
        grid_spec=pltpu.PrefetchScalarGridSpec(
            num_scalar_prefetch=1,
            grid=(spans,),
            in_specs=[
                pl.BlockSpec((nctx, None, ORDER, tiles, 128), lambda h, s: (0, h, 0, 0, 0)),
                pl.BlockSpec((None, ORDER, tiles, 128), lambda h, s: (h, 0, 0, 0)),
                pl.BlockSpec((None, ORDER, tiles, 128), lambda h, s: (h, 0, 0, 0)),
                pl.BlockSpec((length, span), lambda h, s: (0, h)),
                pl.BlockSpec((length, span), lambda h, s: (0, h)),
                pl.BlockSpec((1, span), lambda h, s: (0, h)),
            ],
            out_specs=[
                pl.BlockSpec((length, span), lambda h, s: (0, h)),
                pl.BlockSpec((length, span), lambda h, s: (0, h)),
                pl.BlockSpec((length, 128), lambda h, s: (0, 0)),
            ],
            scratch_shapes=[pltpu.VMEM((length * tiles, 128), jnp.float32)],
        ),
        out_shape=[
            jax.ShapeDtypeStruct((length, here), jnp.bfloat16),
            jax.ShapeDtypeStruct((length, here), jnp.bfloat16),
            jax.ShapeDtypeStruct((length, 128), jnp.float32),
        ],
        name="modal_finish",
    )(rank[None], states, decay_tiles, residue_tiles, query, base, attn_gain[None])
    scaled_full, energy_parts = gather_square("ch", scaled, packed(jnp.sum(lanes, axis=1)), 3)
    stream_energy = jnp.sum(energy_parts, axis=0).reshape(-1)[:length]
    row_scale = lax.rsqrt(stream_energy / D + 1e-06)[:, None]
    projected = (
        jnp.dot(scaled_full, weights_full, preferred_element_type=jnp.float32) * row_scale
    )
    half_dim = HEAD_DIM // 2
    positions = rank * length + jnp.arange(length, dtype=jnp.int32)
    frequency = 10000.0 ** (-(jnp.arange(half_dim, dtype=jnp.float32) / half_dim))
    angle = positions.astype(jnp.float32)[:, None] * frequency[None, :]
    cosine, sine = jnp.cos(angle), jnp.sin(angle)
    width = HEAD_DIM
    qkv = jnp.concatenate(
        [
            rotate(projected[:, :width], cosine, sine),
            rotate(projected[:, width : 2 * width], cosine, sine),
            projected[:, 2 * width :],
        ],
        axis=1,
    ).astype(jnp.bfloat16)
    every = gather_paired("ctx", qkv, 4).reshape(nctx * length, 3 * width)
    blocks = lax.dynamic_slice_in_dim(query_order, rank * 2, 2)
    attended = pl.pallas_call(
        attend,
        in_specs=[
            pl.BlockSpec(memory_space=pltpu.SMEM),
            pl.BlockSpec(memory_space=pltpu.VMEM),
        ],
        out_specs=pl.BlockSpec(memory_space=pltpu.VMEM),
        out_shape=jax.ShapeDtypeStruct((length, width), jnp.bfloat16),
        name="attend",
    )(blocks, every)
    return (mixed, attended)


def solution(mesh):
    placed = (
        P("ctx"),
        P(),
        P(None, "ch"),
        P("ch"),
        P(None, None, "ch"),
        P(None, "ch"),
        P(None, "ch"),
        P("ch"),
        P("ch"),
        P("ctx", "ch"),
    )
    return jax.shard_map(
        shards,
        mesh=mesh,
        in_specs=placed,
        out_specs=(P("ctx", "ch"), P("ctx", "ch")),
        check_vma=False,
    )
```

```python
import functools
import math

import jax
import jax.numpy as jnp
from jax import lax
from jax.experimental import pallas as pl
from jax.experimental.pallas import tpu as pltpu
from jax.sharding import PartitionSpec as P

D = 8192
HEAD_DIM = 128
SHORT = 3
ORDER = 16
HALO = 16
SPAN_MOST = 1024


def modal_local(
    ids_ref,
    scale_ref,
    table_ref,
    gain_ref,
    taps_ref,
    decay_ref,
    residue_ref,
    skip_ref,
    query_ref,
    base_ref,
    state_ref,
    normed_ref,
    gated_ref,
    long_ref,
):
    rows = query_ref.shape[0]
    vocab, span = table_ref.shape
    tiles = span // 128
    padded = ids_ref.shape[0]
    onehot = (
        (ids_ref[...] == lax.broadcasted_iota(jnp.int32, (padded, vocab), 1))
        .astype(jnp.float32)
        .astype(jnp.bfloat16)
    )
    embedded = jnp.dot(onehot, table_ref[...], preferred_element_type=jnp.float32)
    base_ref[...] = embedded[HALO:]
    normed_ref[...] = (
        (embedded * scale_ref[...] * gain_ref[...]).astype(jnp.bfloat16).astype(jnp.float32)
    )
    taps = taps_ref[...]

    def stream(j):
        total = taps[3 * j : 3 * j + 1] * normed_ref[HALO:]
        for i in range(1, SHORT):
            k = 3 * j + i
            total = total + taps[k : k + 1] * normed_ref[HALO - i : HALO - i + rows]
        return total

    query = stream(0)
    gated = stream(1) * stream(2)
    query_ref[...] = query
    base_ref[...] += query * (skip_ref[...] * gated)
    for r in range(rows // 8):
        for k in range(tiles):
            gated_ref[(r * tiles + k) * 8 : (r * tiles + k + 1) * 8, :] = gated[
                r * 8 : r * 8 + 8, k * 128 : k * 128 + 128
            ]
    decay = [jnp.exp(-decay_ref[n]) for n in range(ORDER)]

    def step(r, states):
        states = list(states)
        for t in range(8):
            place = pl.ds(r * (8 * tiles) + t, tiles, stride=8)
            entry = gated_ref[place, :]
            terms = []
            for n in range(ORDER):
                states[n] = decay[n] * states[n] + entry
                terms.append(residue_ref[n] * states[n])
            while len(terms) > 1:
                terms = [a + b for a, b in zip(terms[::2], terms[1::2])]
            long_ref[place, :] = terms[0]
        return tuple(states)

    zero = jnp.zeros((tiles, 128), jnp.float32)
    states = lax.fori_loop(0, rows // 8, step, (zero,) * ORDER)
    for n in range(ORDER):
        state_ref[n] = states[n].astype(state_ref.dtype)
    for r in range(rows // 8):
        for k in range(tiles):
            spot = (slice(r * 8, r * 8 + 8), slice(k * 128, k * 128 + 128))
            base_ref[spot] += (
                query_ref[spot] * long_ref[(r * tiles + k) * 8 : (r * tiles + k + 1) * 8, :]
            )


def modal_finish(
    rank_ref,
    states_ref,
    decay_ref,
    residue_ref,
    query_ref,
    base_ref,
    gain_ref,
    mixed_ref,
    scaled_ref,
    energy_ref,
    long_ref,
):
    rows, span = query_ref.shape
    tiles = span // 128
    rank = rank_ref[0]
    block_decay = [jnp.exp(-decay_ref[n] * float(rows)) for n in range(ORDER)]

    def carry(k, states):
        return tuple(states[n] * block_decay[n] + states_ref[k, n].astype(jnp.float32) for n in range(ORDER))

    zero = jnp.zeros((tiles, 128), jnp.float32)
    incoming = lax.fori_loop(0, rank, carry, (zero,) * ORDER)
    decay = [jnp.exp(-decay_ref[n]) for n in range(ORDER)]

    def step(r, terms):
        terms = list(terms)
        for t in range(8):
            terms = [decay[n] * terms[n] for n in range(ORDER)]
            sums = terms
            while len(sums) > 1:
                sums = [a + b for a, b in zip(sums[::2], sums[1::2])]
            long_ref[pl.ds(r * (8 * tiles) + t, tiles, stride=8), :] = sums[0]
        return tuple(terms)

    lax.fori_loop(
        0, rows // 8, step, tuple(residue_ref[n] * incoming[n] for n in range(ORDER))
    )

    @pl.when(pl.program_id(0) == 0)
    def _():
        energy_ref[...] = jnp.zeros_like(energy_ref)

    for r in range(rows // 16):
        energy = jnp.zeros((16, 128), jnp.float32)
        for k in range(tiles):
            spot = (slice(r * 16, r * 16 + 16), slice(k * 128, k * 128 + 128))
            first = (2 * r * tiles + k) * 8
            second = ((2 * r + 1) * tiles + k) * 8
            late = jnp.concatenate(
                [long_ref[first : first + 8, :], long_ref[second : second + 8, :]], axis=0
            )
            mixed = (base_ref[spot] + query_ref[spot] * late).astype(jnp.bfloat16)
            mixed_ref[spot] = mixed
            wide = mixed.astype(jnp.float32)
            scaled_ref[spot] = (wide * gain_ref[:, spot[1]]).astype(jnp.bfloat16)
            energy = energy + wide * wide
        energy_ref[r * 16 : r * 16 + 16, :] += energy


def direct_kernel(axis, columns, count, *refs):
    ins, outs = refs[:count], refs[count : 2 * count]
    send, recv, own = refs[2 * count :]
    size, me = lax.axis_size(axis), lax.axis_index(axis)
    barrier = pltpu.get_barrier_semaphore()
    for d in range(1, size):
        peer = lax.rem(me + d, size)
        pl.semaphore_signal(
            barrier, inc=1, device_id={axis: peer}, device_id_type=pl.DeviceIdType.MESH
        )
    pl.semaphore_wait(barrier, size - 1)
    copies = []
    for a in range(count):
        if columns[a]:
            width = ins[a].shape[1]
            spot = outs[a].at[:, pl.ds(pl.multiple_of(me * width, 128), width)]
        else:
            spot = outs[a].at[me]
        for d in range(1, size):
            copies.append(
                pltpu.make_async_remote_copy(
                    src_ref=ins[a],
                    dst_ref=spot,
                    send_sem=send.at[a, d - 1],
                    recv_sem=recv.at[a, d - 1],
                    device_id={axis: lax.rem(me + d, size)},
                    device_id_type=pl.DeviceIdType.MESH,
                )
            )
        copies.append(pltpu.make_async_copy(ins[a], spot, own.at[a]))
    for copy in copies:
        copy.start()
    for copy in copies:
        copy.wait()


def square_kernel(
    axis, in_ref, small_ref, out_ref, small_out_ref, send, recv, small_send, small_recv, own
):
    me = lax.axis_index(axis)
    y, x = lax.div(me, 2), lax.rem(me, 2)
    beside, above = y * 2 + 1 - x, (1 - y) * 2 + x
    peers = [beside, above, (1 - y) * 2 + 1 - x]
    barrier = pltpu.get_barrier_semaphore()
    for peer in peers:
        pl.semaphore_signal(
            barrier, inc=1, device_id={axis: peer}, device_id_type=pl.DeviceIdType.MESH
        )
    pl.semaphore_wait(barrier, 3)
    rows, width = in_ref.shape
    half = rows // 2

    def spot(owner, part):
        return out_ref.at[
            part * half : (part + 1) * half, pl.ds(pl.multiple_of(owner * width, 128), width)
        ]

    def remote(source, target, slot, peer):
        return pltpu.make_async_remote_copy(
            src_ref=source,
            dst_ref=target,
            send_sem=send.at[slot],
            recv_sem=recv.at[slot],
            device_id={axis: peer},
            device_id_type=pl.DeviceIdType.MESH,
        )

    parts = [in_ref.at[:half], in_ref.at[half:]]
    first = remote(parts[0], spot(me, 0), 0, beside)
    second = remote(parts[1], spot(me, 1), 1, above)
    third = remote(parts[1], spot(me, 1), 2, beside)
    fourth = remote(parts[0], spot(me, 0), 3, above)
    small = [
        pltpu.make_async_remote_copy(
            src_ref=small_ref,
            dst_ref=small_out_ref.at[me],
            send_sem=small_send.at[d],
            recv_sem=small_recv.at[d],
            device_id={axis: peers[d]},
            device_id_type=pl.DeviceIdType.MESH,
        )
        for d in range(3)
    ]
    mine = [
        pltpu.make_async_copy(parts[0], spot(me, 0), own.at[0]),
        pltpu.make_async_copy(parts[1], spot(me, 1), own.at[1]),
        pltpu.make_async_copy(small_ref, small_out_ref.at[me], own.at[2]),
    ]
    for copy in [first, second] + small + [third, fourth] + mine:
        copy.start()
    first.wait_recv()
    onward = remote(spot(beside, 0), spot(beside, 0), 4, above)
    onward.start()
    second.wait_recv()
    across = remote(spot(above, 1), spot(above, 1), 5, beside)
    across.start()
    first.wait_send()
    second.wait_send()
    for copy in [third, fourth] + small + mine + [onward, across]:
        copy.wait()


def paired_kernel(axis, pieces, in_ref, out_ref, send, recv, hand_send, hand_recv, own):
    size, me = lax.axis_size(axis), lax.axis_index(axis)
    chips = size // 2
    chip, core = lax.div(me, 2), lax.rem(me, 2)
    sibling = me + 1 - 2 * core
    ways = ((1, chip < chips - 1), (-1, chip > 0))
    barrier = pltpu.get_barrier_semaphore()

    def greet(peer):
        pl.semaphore_signal(
            barrier, inc=1, device_id={axis: peer}, device_id_type=pl.DeviceIdType.MESH
        )

    greet(sibling)
    for way, open_ in ways:
        pl.when(open_)(functools.partial(greet, me + 2 * way))
    for count in (2, 3):
        inner = (chip > 0) & (chip < chips - 1)
        pl.when(inner if count == 3 else jnp.logical_not(inner))(
            functools.partial(pl.semaphore_wait, barrier, count)
        )
    rows = in_ref.shape[0] // pieces

    def remote(source, owner, part, sends, recvs, spot, peer):
        return pltpu.make_async_remote_copy(
            src_ref=source,
            dst_ref=out_ref.at[owner, part * rows : (part + 1) * rows],
            send_sem=sends.at[spot],
            recv_sem=recvs.at[spot],
            device_id={axis: peer},
            device_id_type=pl.DeviceIdType.MESH,
        )

    def block(owner, part):
        return out_ref.at[owner, part * rows : (part + 1) * rows]

    def outgoing(w, d, part):
        way = ways[w][0]
        owner = me - 2 * way * (d - 1)
        source = in_ref.at[part * rows : (part + 1) * rows] if d == 1 else block(owner, part)
        return remote(source, owner, part, send, recv, (w, d - 1, part), me + 2 * way)

    def incoming(w, d, part):
        owner = me - 2 * ways[w][0] * d
        return remote(
            block(owner, part), owner, part, send, recv, (w, d - 1, part), sibling
        )

    def handed(w, d, part):
        owner = me - 2 * ways[w][0] * d
        return remote(
            block(owner, part), owner, part, hand_send, hand_recv, (w, d, part), sibling
        )

    def arrives(w, d):
        return chip >= d if w == 0 else chip + d < chips

    for part in range(pieces):
        for w in range(2):
            pl.when(ways[w][1])(lambda w=w, part=part: outgoing(w, 1, part).start())
    for part in range(pieces):
        remote(
            in_ref.at[part * rows : (part + 1) * rows],
            me,
            part,
            hand_send,
            hand_recv,
            (0, 0, part),
            sibling,
        ).start()
    mine = pltpu.make_async_copy(in_ref, out_ref.at[me], own)
    mine.start()

    def relay(w, d, part):
        incoming(w, d, part).wait_recv()
        if d < chips - 1:
            pl.when(ways[w][1])(lambda: outgoing(w, d + 1, part).start())
        handed(w, d, part).start()

    for d in range(1, chips):
        for part in range(pieces):
            for w in range(2):
                pl.when(arrives(w, d))(functools.partial(relay, w, d, part))
    mine.wait()
    for part in range(pieces):
        remote(
            in_ref.at[part * rows : (part + 1) * rows],
            me,
            part,
            hand_send,
            hand_recv,
            (0, 0, part),
            sibling,
        ).wait()
        for w in range(2):
            pl.when(ways[w][1])(lambda w=w, part=part: outgoing(w, 1, part).wait_send())
            for d in range(1, chips):

                def finish(w=w, d=d, part=part):
                    handed(w, d, part).wait()
                    if d < chips - 1:
                        pl.when(ways[w][1])(lambda: outgoing(w, d + 1, part).wait_send())

                pl.when(arrives(w, d))(finish)


def star_kernel(axis, in_ref, out_ref, send, recv, hand_send, hand_recv, own):
    size, me = lax.axis_size(axis), lax.axis_index(axis)
    chips = size // 2
    chip, core = lax.div(me, 2), lax.rem(me, 2)
    sibling = me + 1 - 2 * core
    peers = [sibling] + [lax.rem(chip + d, chips) * 2 + core for d in range(1, chips)]
    barrier = pltpu.get_barrier_semaphore()
    for peer in peers:
        pl.semaphore_signal(
            barrier, inc=1, device_id={axis: peer}, device_id_type=pl.DeviceIdType.MESH
        )
    pl.semaphore_wait(barrier, chips)
    copies = [
        pltpu.make_async_remote_copy(
            src_ref=in_ref,
            dst_ref=out_ref.at[me],
            send_sem=send.at[d],
            recv_sem=recv.at[d],
            device_id={axis: peers[d]},
            device_id_type=pl.DeviceIdType.MESH,
        )
        for d in range(chips)
    ]
    for copy in copies[1:]:
        copy.start()
    copies[0].start()
    mine = pltpu.make_async_copy(in_ref, out_ref.at[me], own)
    mine.start()
    hands = []
    for d in range(1, chips):
        copies[d].wait_recv()
        source = lax.rem(chip + chips - d, chips) * 2 + core
        hand = pltpu.make_async_remote_copy(
            src_ref=out_ref.at[source],
            dst_ref=out_ref.at[source],
            send_sem=hand_send.at[d],
            recv_sem=hand_recv.at[d],
            device_id={axis: sibling},
            device_id_type=pl.DeviceIdType.MESH,
        )
        hand.start()
        hands.append(hand)
    mine.wait()
    copies[0].wait_recv()
    for copy in copies:
        copy.wait_send()
    for hand in hands:
        hand.wait()


def gather_direct(axis, arrays, columns, collective_id):
    size, count = lax.axis_size(axis), len(arrays)
    vmem = pl.BlockSpec(memory_space=pltpu.VMEM)
    dma = pltpu.SemaphoreType.DMA
    return pl.pallas_call(
        functools.partial(direct_kernel, axis, columns, count),
        in_specs=[vmem] * count,
        out_specs=[vmem] * count,
        out_shape=[
            jax.ShapeDtypeStruct(
                (a.shape[0], size * a.shape[1]) if wide else (size,) + a.shape, a.dtype
            )
            for a, wide in zip(arrays, columns)
        ],
        scratch_shapes=[dma((count, size - 1)), dma((count, size - 1)), dma((count,))],
        compiler_params=pltpu.CompilerParams(
            collective_id=collective_id, has_side_effects=True
        ),
    )(*arrays)


def gather_square(axis, array, small, collective_id):
    size = lax.axis_size(axis)
    if size != 4:
        return gather_direct(axis, [array, small], (True, False), collective_id)
    vmem = pl.BlockSpec(memory_space=pltpu.VMEM)
    dma = pltpu.SemaphoreType.DMA
    return pl.pallas_call(
        functools.partial(square_kernel, axis),
        in_specs=[vmem, vmem],
        out_specs=[vmem, vmem],
        out_shape=[
            jax.ShapeDtypeStruct((array.shape[0], size * array.shape[1]), array.dtype),
            jax.ShapeDtypeStruct((size,) + small.shape, small.dtype),
        ],
        scratch_shapes=[dma((6,)), dma((6,)), dma((3,)), dma((3,)), dma((3,))],
        compiler_params=pltpu.CompilerParams(
            collective_id=collective_id, has_side_effects=True
        ),
    )(array, small)


def gather_paired(axis, array, collective_id):
    size = lax.axis_size(axis)
    vmem = pl.BlockSpec(memory_space=pltpu.VMEM)
    dma = pltpu.SemaphoreType.DMA
    chips, pieces = size // 2, 2
    return pl.pallas_call(
        functools.partial(paired_kernel, axis, pieces),
        in_specs=[vmem],
        out_specs=vmem,
        out_shape=jax.ShapeDtypeStruct((size,) + array.shape, array.dtype),
        scratch_shapes=[dma((2, chips, pieces))] * 4 + [dma(())],
        compiler_params=pltpu.CompilerParams(
            collective_id=collective_id, has_side_effects=True
        ),
    )(array)


def gather_star(axis, array, collective_id):
    size = lax.axis_size(axis)
    vmem = pl.BlockSpec(memory_space=pltpu.VMEM)
    dma = pltpu.SemaphoreType.DMA
    chips = size // 2
    return pl.pallas_call(
        functools.partial(star_kernel, axis),
        in_specs=[vmem],
        out_specs=vmem,
        out_shape=jax.ShapeDtypeStruct((size,) + array.shape, array.dtype),
        scratch_shapes=[dma((chips,)), dma((chips,)), dma((chips,)), dma((chips,)), dma(())],
        compiler_params=pltpu.CompilerParams(
            collective_id=collective_id, has_side_effects=True
        ),
    )(array)


def packed(vector):
    wide = -(-vector.shape[0] // 1024) * 1024
    return jnp.pad(vector, (0, wide - vector.shape[0])).reshape(wide // 128, 128)


def attend(blocks_ref, qkv_ref, out_ref):
    half_rows = out_ref.shape[0] // 2
    keys_total = qkv_ref.shape[0]
    width = HEAD_DIM
    for b in range(2):
        start = pl.multiple_of(blocks_ref[b] * half_rows, 32)
        queries = qkv_ref[pl.ds(start, half_rows), :width]
        keys = qkv_ref[:, width : 2 * width]
        values = qkv_ref[:, 2 * width :]
        scores = lax.dot_general(
            queries, keys, (((1,), (1,)), ((), ())), preferred_element_type=jnp.float32
        ) * (1.0 / math.sqrt(HEAD_DIM))
        at = start + lax.broadcasted_iota(jnp.int32, (half_rows, keys_total), 0)
        allowed = lax.broadcasted_iota(jnp.int32, (half_rows, keys_total), 1) <= at
        masked = jnp.where(allowed, scores, -1e30)
        top = jnp.max(masked, axis=1, keepdims=True)
        weights = jnp.where(allowed, jnp.exp(masked - top), 0.0)
        total = jnp.sum(weights, axis=1, keepdims=True)
        out = jnp.dot(weights.astype(jnp.bfloat16), values, preferred_element_type=jnp.float32)
        out_ref[b * half_rows : (b + 1) * half_rows, :] = (out / total).astype(jnp.bfloat16)


def rotate(vectors, cosine, sine):
    half_dim = HEAD_DIM // 2
    first = vectors[:, :half_dim]
    second = vectors[:, half_dim:]
    return jnp.concatenate(
        [first * cosine - second * sine, second * cosine + first * sine], axis=1
    )


def shards(
    token_ids,
    query_order,
    embed_table,
    hyena_gain,
    short_filter,
    decay_rate,
    residue,
    skip_gain,
    attn_gain,
    w_qkv,
):
    length = token_ids.shape[0]
    vocab = embed_table.shape[0]
    here = embed_table.shape[1]
    span = min(SPAN_MOST, here)
    spans = here // span
    tiles = span // 128
    nctx = lax.axis_size("ctx")
    rank = lax.axis_index("ctx")
    padded = length + HALO
    weights_full = lax.all_gather(w_qkv, "ctx", axis=0, tiled=True)
    earlier_ids = lax.ppermute(
        token_ids[length - HALO :], "ctx", [(i, i + 1) for i in range(nctx - 1)]
    )
    ids = jnp.concatenate([earlier_ids, token_ids])
    table_wide = embed_table.astype(jnp.float32)
    (table_parts,) = gather_direct(
        "ch", [packed(jnp.sum(table_wide * table_wide, axis=1))], (False,), 1
    )
    table_energy = jnp.sum(table_parts, axis=0).reshape(-1)[:vocab]
    energy = jnp.sum(
        jnp.where(
            ids[:, None] == jnp.arange(vocab, dtype=jnp.int32)[None, :], table_energy[None, :], 0.0
        ),
        axis=1,
    )
    real = (jnp.arange(padded) >= HALO) | (rank > 0)
    scale = jnp.where(real, lax.rsqrt(energy / D + 1e-06), 0.0)
    decay_tiles = decay_rate.reshape(ORDER, spans, tiles, 128).swapaxes(0, 1)
    residue_tiles = residue.reshape(ORDER, spans, tiles, 128).swapaxes(0, 1)
    row = lambda size: pl.BlockSpec((size, span), lambda h: (0, h))
    tile = pl.BlockSpec((None, ORDER, tiles, 128), lambda h: (h, 0, 0, 0))
    lone = lambda size: pl.BlockSpec((size, 1), lambda h: (0, 0))
    local = pl.pallas_call(
        modal_local,
        grid=(spans,),
        in_specs=[
            lone(padded), lone(padded), row(vocab), row(1), row(9), tile, tile, row(1)
        ],
        out_specs=[row(length), row(length), tile],
        out_shape=[
            jax.ShapeDtypeStruct((length, here), jnp.float32),
            jax.ShapeDtypeStruct((length, here), jnp.float32),
            jax.ShapeDtypeStruct((spans, ORDER, tiles, 128), jnp.bfloat16),
        ],
        scratch_shapes=[
            pltpu.VMEM((padded, span), jnp.float32),
            pltpu.VMEM((length * tiles, 128), jnp.float32),
            pltpu.VMEM((length * tiles, 128), jnp.float32),
        ],
        name="modal_local",
    )
    local_args = (
        ids[:, None],
        scale[:, None],
        embed_table,
        hyena_gain[None],
        short_filter.reshape(9, here),
        decay_tiles,
        residue_tiles,
        skip_gain[None],
    )
    query, base, state = local(*local_args)
    states = gather_star(
        "ctx", state.reshape(spans * ORDER * tiles, 128), 2
    ).reshape(nctx, spans, ORDER, tiles, 128)
    mixed, scaled, lanes = pl.pallas_call(
        modal_finish,
        grid_spec=pltpu.PrefetchScalarGridSpec(
            num_scalar_prefetch=1,
            grid=(spans,),
            in_specs=[
                pl.BlockSpec((nctx, None, ORDER, tiles, 128), lambda h, s: (0, h, 0, 0, 0)),
                pl.BlockSpec((None, ORDER, tiles, 128), lambda h, s: (h, 0, 0, 0)),
                pl.BlockSpec((None, ORDER, tiles, 128), lambda h, s: (h, 0, 0, 0)),
                pl.BlockSpec((length, span), lambda h, s: (0, h)),
                pl.BlockSpec((length, span), lambda h, s: (0, h)),
                pl.BlockSpec((1, span), lambda h, s: (0, h)),
            ],
            out_specs=[
                pl.BlockSpec((length, span), lambda h, s: (0, h)),
                pl.BlockSpec((length, span), lambda h, s: (0, h)),
                pl.BlockSpec((length, 128), lambda h, s: (0, 0)),
            ],
            scratch_shapes=[pltpu.VMEM((length * tiles, 128), jnp.float32)],
        ),
        out_shape=[
            jax.ShapeDtypeStruct((length, here), jnp.bfloat16),
            jax.ShapeDtypeStruct((length, here), jnp.bfloat16),
            jax.ShapeDtypeStruct((length, 128), jnp.float32),
        ],
        name="modal_finish",
    )(rank[None], states, decay_tiles, residue_tiles, query, base, attn_gain[None])
    scaled_full, energy_parts = gather_square("ch", scaled, packed(jnp.sum(lanes, axis=1)), 3)
    stream_energy = jnp.sum(energy_parts, axis=0).reshape(-1)[:length]
    row_scale = lax.rsqrt(stream_energy / D + 1e-06)[:, None]
    projected = (
        jnp.dot(scaled_full, weights_full, preferred_element_type=jnp.float32) * row_scale
    )
    half_dim = HEAD_DIM // 2
    positions = rank * length + jnp.arange(length, dtype=jnp.int32)
    frequency = 10000.0 ** (-(jnp.arange(half_dim, dtype=jnp.float32) / half_dim))
    angle = positions.astype(jnp.float32)[:, None] * frequency[None, :]
    cosine, sine = jnp.cos(angle), jnp.sin(angle)
    width = HEAD_DIM
    qkv = jnp.concatenate(
        [
            rotate(projected[:, :width], cosine, sine),
            rotate(projected[:, width : 2 * width], cosine, sine),
            projected[:, 2 * width :],
        ],
        axis=1,
    ).astype(jnp.bfloat16)
    every = gather_paired("ctx", qkv, 4).reshape(nctx * length, 3 * width)
    blocks = lax.dynamic_slice_in_dim(query_order, rank * 2, 2)
    attended = pl.pallas_call(
        attend,
        in_specs=[
            pl.BlockSpec(memory_space=pltpu.SMEM),
            pl.BlockSpec(memory_space=pltpu.VMEM),
        ],
        out_specs=pl.BlockSpec(memory_space=pltpu.VMEM),
        out_shape=jax.ShapeDtypeStruct((length, width), jnp.bfloat16),
        name="attend",
    )(blocks, every)
    return (mixed, attended)


def solution(mesh):
    placed = (
        P("ctx"),
        P(),
        P(None, "ch"),
        P("ch"),
        P(None, None, "ch"),
        P(None, "ch"),
        P(None, "ch"),
        P("ch"),
        P("ch"),
        P("ctx", "ch"),
    )
    return jax.shard_map(
        shards,
        mesh=mesh,
        in_specs=placed,
        out_specs=(P("ctx", "ch"), P("ctx", "ch")),
        check_vma=False,
    )
```
